32 devices in a mesh: angle: 2 (over y), tile: 8 (over z, core), layer: 2 (over x).
Axes of the slice: x: 2, y: 2, z: 4, core: 2. Of those that a mesh axis runs over, the one named last changes fastest.
Arguments:
- frames: bfloat16 [2, 1024, 192, 512], P('layer', 'angle', 'tile'), may hold values from 0.0625 to 8, as said below
- exponents: int32 [2, 1024, 192, 4], P('layer', 'angle', 'tile'), may hold values from -1 to 1
- valid_mask: int32 [2, 192, 512], P('layer', 'tile', 'angle'), may hold values 0 or 1
Outputs:
- orientation: float32 [2, 2, 192, 512], P(None, 'layer', 'tile', 'angle')
- spread: float32 [3, 2, 192, 512], P(None, 'layer', 'tile', 'angle')
- nye_tensor: float32 [7, 2, 192, 512], P(None, 'layer', 'tile', 'angle')
The draws below stay inside these ranges and needn't reach their ends.
Inputs may be any that keep to these rules, and one draw needn't show every extreme that they name: `frames`: positive intensities.
All inputs are finite; a program needn't handle non-finite values. No bound on the sum of `valid_mask` on one device may be relied on, other than what follows from the above.
Results may differ from the reference program's by a relative error of at most 0.0003.
Values sent between devices are 32-bit elements; how exact they have to be, the bound alone decides.
No kernel may reach another device: no remote copies, remote signals or barrier semaphores. Data moves between devices by JAX's collectives and lax.ppermute only.
A program may use at most 128 MiB of HBM per device.

```python
import math
import jax
import jax.numpy as jnp
from jax import lax

NPHI = 32
NCHI = 32
QBLK = 128
ROWS_DEV = 24
ANGLES = 1024
LAYERS = 2
ROWS = 192
COLS = 512


def draw_frames(key, part):
    subkeys = jax.random.split(jax.random.fold_in(key, 17), 5)
    pixel_shape = (LAYERS, 1, ROWS, COLS)
    position = jnp.arange(ANGLES, dtype=jnp.int32)
    phi_coord = ((position // NCHI).astype(jnp.float32) - 0.5 * (NPHI - 1)) / (0.5 * NPHI)
    chi_coord = ((position % NCHI).astype(jnp.float32) - 0.5 * (NCHI - 1)) / (0.5 * NCHI)
    phi_coord = phi_coord.reshape(1, ANGLES, 1, 1)
    chi_coord = chi_coord.reshape(1, ANGLES, 1, 1)
    extent = 0.6
    narrowest = 0.12
    broadest = 0.4
    height = jnp.exp(jax.random.uniform(subkeys[2], pixel_shape, minval=math.log(2.0), maxval=math.log(40.0)))
    centre_phi = jax.random.uniform(subkeys[0], pixel_shape, minval=-extent, maxval=extent)
    centre_chi = jax.random.uniform(subkeys[1], pixel_shape, minval=-extent, maxval=extent)
    breadth = jnp.exp(jax.random.uniform(subkeys[3], pixel_shape, minval=math.log(narrowest), maxval=math.log(broadest)))
    distance = (phi_coord - centre_phi) ** 2 + (chi_coord - centre_chi) ** 2
    profile = height * jnp.exp(-distance / (2.0 * breadth * breadth))
    jitter = jax.random.uniform(subkeys[4], (LAYERS, ANGLES, ROWS, COLS))
    result = profile * (0.7 + 0.6 * jitter) + 0.05 + 0.25 * (1.0 - jitter)
    return jnp.clip(result, 0.0625, 8.0).astype(jnp.bfloat16)


def touch_ends(values, own_key, least, largest):
    longest = values.shape.index(max(values.shape))
    spots = []
    for shift in (0, 1):
        where = [jax.random.randint(jax.random.fold_in(own_key, axis), (), 0, length) for axis, length in enumerate(values.shape)]
        where[longest] = (where[longest] + shift) % values.shape[longest]
        spots.append(tuple(where))
    return values.at[spots[0]].set(least).at[spots[1]].set(largest)


def setup_inputs(seed: int = 0) -> dict:
    streams_of = jax.random.split(jax.random.key(seed), 4)
    return {
        "frames": draw_frames(jax.random.fold_in(streams_of[3], 71), 0),
        "exponents": touch_ends(jax.random.randint(streams_of[1], (LAYERS, ANGLES, ROWS, COLS // QBLK), -1, 2), jax.random.fold_in(streams_of[1], 1), -1, 1).astype(jnp.int32),
        "valid_mask": touch_ends((jax.random.randint(streams_of[2], (LAYERS, ROWS, COLS), 0, 8) < 7).astype(jnp.int32), jax.random.fold_in(streams_of[2], 1), 0, 1),
    }


layer_pitch = 2.0


def angle_table(first_angle, count_angles):
    position = first_angle + jnp.arange(count_angles, dtype=jnp.int32)
    phi_index = (position // NCHI).astype(jnp.float32)
    chi_index = (position % NCHI).astype(jnp.float32)
    phi_coord = (phi_index - 0.5 * (NPHI - 1)) / (0.5 * NPHI)
    chi_coord = (chi_index - 0.5 * (NCHI - 1)) / (0.5 * NCHI)
    constant = jnp.ones_like(phi_coord)
    return jnp.stack([constant, phi_coord, chi_coord, phi_coord * phi_coord,
                      chi_coord * chi_coord, phi_coord * chi_coord]).astype(jnp.bfloat16)


def intensity_of(frames, exponents):
    layers_here, angles_here, rows_here, columns = frames.shape
    blocks = exponents.shape[3]
    factor = jnp.exp2(exponents.astype(jnp.float32)).astype(jnp.bfloat16)
    scaled = frames.reshape(layers_here, angles_here, rows_here, blocks, columns // blocks) * factor[..., None]
    return scaled.reshape(layers_here, angles_here, rows_here * columns)


def orientation_of(moments):
    zeroth = moments[0]
    return jnp.stack([moments[1] / zeroth, moments[2] / zeroth])


def spread_of(moments, orient):
    zeroth = moments[0]
    return jnp.stack([moments[3] / zeroth - orient[0] * orient[0],
                      moments[4] / zeroth - orient[1] * orient[1],
                      moments[5] / zeroth - orient[0] * orient[1]])


def nye_of(padded):
    along_x = 0.5 * (padded[:, 1:-1, 1:-1, 2:] - padded[:, 1:-1, 1:-1, :-2])
    along_y = 0.5 * (padded[:, 1:-1, 2:, 1:-1] - padded[:, 1:-1, :-2, 1:-1])
    along_z = (0.5 / layer_pitch) * (padded[:, 2:, 1:-1, 1:-1] - padded[:, :-2, 1:-1, 1:-1])
    trace_sum = along_x[0] + along_y[1]
    return jnp.stack([-along_y[1], -along_x[0], -trace_sum, along_x[1], along_y[0], along_z[0], along_z[1]])


def reference(frames, exponents, valid_mask):
    layers, angles, rows_all, columns = frames.shape
    blocks = exponents.shape[3]
    angle_weights = angle_table(jnp.zeros((), jnp.int32), angles)
    row_block = ROWS_DEV
    row_blocks = rows_all // row_block

    def one_piece(item_index):
        layer_index = item_index // row_blocks
        first_row = (item_index % row_blocks) * row_block
        anchor = jnp.zeros((), jnp.int32)
        frame_piece = lax.dynamic_slice(frames, (layer_index, anchor, first_row, anchor),
                                        (1, angles, row_block, columns))
        scale_piece = lax.dynamic_slice(exponents, (layer_index, anchor, first_row, anchor),
                                        (1, angles, row_block, blocks))
        intensity = intensity_of(frame_piece, scale_piece)[0]
        return jnp.dot(angle_weights, intensity, preferred_element_type=jnp.float32).reshape(6, row_block, columns)

    stacked = lax.map(one_piece, jnp.arange(layers * row_blocks, dtype=jnp.int32))
    moments = stacked.reshape(layers, row_blocks, 6, row_block, columns)
    moments = moments.transpose(2, 0, 1, 3, 4).reshape(6, layers, rows_all, columns)
    orient = orientation_of(moments)
    mask_float = valid_mask.astype(jnp.float32)
    spread = spread_of(moments, orient) * mask_float
    padded = jnp.pad(orient, ((0, 0), (1, 1), (1, 1), (1, 1)))
    nye_tensor = nye_of(padded) * mask_float
    return orient * mask_float, spread, nye_tensor
```

```python
import functools
import jax
import jax.numpy as jnp
from jax import lax
from jax.experimental import pallas as pl
from jax.experimental.pallas import tpu as pltpu
from jax.sharding import PartitionSpec as P

NPHI = 32
NCHI = 32
layer_pitch = 2.0
F32 = jnp.float32
BF16 = jnp.bfloat16
VMEM = pl.BlockSpec(memory_space=pltpu.VMEM)
ANY = pl.BlockSpec(memory_space=pl.ANY)


def moments_body(shift, count, steps, e_hbm, f_hbm, low_ref, high_ref, buf, ebuf, sem, esem):
    angles, rows, width = buf.shape
    blocks = ebuf.shape[1]
    span = f_hbm.shape[2] // blocks
    here = width // span
    deep = NCHI * 8
    me = lax.axis_index("angle")
    block = lax.rem(me + shift, count)
    column = pl.multiple_of(block * width, width)
    exponent_copy = pltpu.make_async_copy(e_hbm, ebuf, esem)
    exponent_copy.start()
    size = angles // steps
    copies = []
    for step in range(steps):
        part = pl.ds(step * size, size)
        copy = pltpu.make_async_copy(
            f_hbm.at[part, :, pl.ds(column, width)], buf.at[part], sem.at[step]
        )
        copy.start()
        copies.append(copy)
    low_ref[...] = jnp.zeros_like(low_ref)
    high_ref[...] = jnp.zeros_like(high_ref)
    lane = lax.broadcasted_iota(jnp.int32, (8, deep), 1)
    diagonal = (lane & 7) == lax.broadcasted_iota(jnp.int32, (8, deep), 0)
    chi = ((lane >> 3).astype(F32) - 0.5 * (NCHI - 1)) / (0.5 * NCHI)
    chi_chi = (chi * chi).astype(BF16).astype(F32)
    source = lax.broadcasted_iota(jnp.int32, (128, deep), 0)
    target = lax.broadcasted_iota(jnp.int32, (128, deep), 1) >> 3
    spread_out = [
        (source == target + NCHI * part).astype(F32).astype(BF16) for part in range(128 // NCHI)
    ]
    exponent_copy.wait()
    factor = jnp.concatenate(
        [
            jnp.exp2(ebuf[:, pl.ds(block * here + b, 1), :].reshape(rows, angles).astype(F32))
            for b in range(here)
        ],
        0,
    ).astype(BF16)
    first_phi = me * (angles // NCHI)
    for g in range(angles // NCHI):
        if (g * NCHI) % size == 0:
            copies[(g * NCHI) // size].wait()
        chunk = g * NCHI // 128 * 128
        factors = jnp.dot(
            factor[:, chunk : chunk + 128],
            spread_out[g % (128 // NCHI)],
            preferred_element_type=F32,
        )
        phi = ((first_phi + g).astype(F32) - 0.5 * (NPHI - 1)) / (0.5 * NPHI)
        phi_chi = (phi * chi).astype(BF16).astype(F32)
        phi_phi = jnp.full((8, 128), phi * phi, F32).astype(BF16).astype(F32)[:, :1]
        for r in range(rows // 8):
            at_rows = slice(r * 8, r * 8 + 8)
            for b in range(here):
                at_columns = slice(b * span, (b + 1) * span)
                top = b * rows + r * 8
                unit = jnp.where(diagonal, factors[top : top + 8], 0.0)
                left = jnp.concatenate([unit, unit * chi, unit * chi_chi, unit * phi_chi], 0)
                cells = buf[g * NCHI : (g + 1) * NCHI, at_rows, at_columns].reshape(deep, span)
                sums = jnp.dot(left.astype(BF16), cells, preferred_element_type=F32)
                low_ref[0, at_rows, at_columns] += sums[:8]
                low_ref[1, at_rows, at_columns] += sums[:8] * phi
                low_ref[2, at_rows, at_columns] += sums[8:16]
                high_ref[0, at_rows, at_columns] += sums[:8] * phi_phi
                high_ref[1, at_rows, at_columns] += sums[16:24]
                high_ref[2, at_rows, at_columns] += sums[24:]


def partial_moments(frames, exponents, shift, count):
    angles, rows, columns = frames.shape
    width = columns // count
    steps = 8
    return pl.pallas_call(
        functools.partial(moments_body, shift, count, steps),
        out_shape=[jax.ShapeDtypeStruct((3, rows, width), F32)] * 2,
        in_specs=[ANY, ANY],
        out_specs=[VMEM, VMEM],
        scratch_shapes=[
            pltpu.VMEM((angles, rows, width), BF16),
            pltpu.VMEM(exponents.shape, jnp.int32),
            pltpu.SemaphoreType.DMA((steps,)),
            pltpu.SemaphoreType.DMA,
        ],
        name=f"moments_{shift}",
        cost_estimate=pl.CostEstimate(
            flops=512 * angles * rows * width,
            bytes_accessed=2 * angles * rows * width,
            transcendentals=0,
        ),
    )(exponents, frames)


def field_body(count, own_ref, *refs):
    parts, (field_ref, even_ref, odd_ref) = refs[: count - 1], refs[count - 1 :]
    total = own_ref[...]
    for part in parts:
        total = total + part[...]
    first = total[1] / total[0]
    second = total[2] / total[0]
    field_ref[0] = first
    field_ref[1] = second
    rows = first.shape[0]
    is_even = lax.rem(lax.axis_index("tile"), 2) == 0
    for c, value in ((0, first), (1, second)):
        head, tail = value[:1], value[rows - 1 :]
        even_ref[c] = jnp.where(is_even, tail, head)
        odd_ref[c] = jnp.where(is_even, head, tail)


def field_of(own, parts):
    _, rows, width = own.shape
    edge = jax.ShapeDtypeStruct((2, 1, width), F32)
    return pl.pallas_call(
        functools.partial(field_body, len(parts) + 1),
        out_shape=[jax.ShapeDtypeStruct((2, rows, width), F32), edge, edge],
        in_specs=[VMEM] * (len(parts) + 1),
        out_specs=[VMEM] * 3,
        name="field",
    )(own, *parts)


def spread_body(count, mask_ref, field_ref, low_ref, high_ref, *refs):
    parts, (orient_ref, spread_ref) = refs[: 2 * count - 2], refs[2 * count - 2 :]
    mask = mask_ref[0].astype(F32)
    zeroth = low_ref[0]
    seconds = high_ref[...]
    for k in range(count - 1):
        zeroth = zeroth + parts[2 * k][0]
        seconds = seconds + parts[2 * k + 1][...]
    first, second = field_ref[0], field_ref[1]
    orient_ref[0, 0] = first * mask
    orient_ref[1, 0] = second * mask
    spread_ref[0, 0] = (seconds[0] / zeroth - first * first) * mask
    spread_ref[1, 0] = (seconds[1] / zeroth - second * second) * mask
    spread_ref[2, 0] = (seconds[2] / zeroth - first * second) * mask


def spread_of(mask, field, low, high, parts):
    _, rows, width = field.shape
    flat = [x for pair in parts for x in pair]
    return pl.pallas_call(
        functools.partial(spread_body, len(parts) + 1),
        out_shape=[
            jax.ShapeDtypeStruct((2, 1, rows, width), F32),
            jax.ShapeDtypeStruct((3, 1, rows, width), F32),
        ],
        in_specs=[VMEM] * (4 + len(flat)),
        out_specs=[VMEM] * 2,
        name="spread",
    )(mask, field, low, high, *flat)


def nye_body(mask_ref, field_ref, even_ref, odd_ref, left_ref, right_ref, below_ref, above_ref, nye_ref):
    rows, width = field_ref.shape[1:]
    mask = mask_ref[0].astype(F32)
    is_even = lax.rem(lax.axis_index("tile"), 2) == 0
    row = lax.broadcasted_iota(jnp.int32, (rows, width), 0)
    column = lax.broadcasted_iota(jnp.int32, (rows, width), 1)
    along_x, along_y, along_z = [], [], []
    for c in range(2):
        value = field_ref[c]
        upper = jnp.where(is_even, odd_ref[c], even_ref[c])
        lower = jnp.where(is_even, even_ref[c], odd_ref[c])
        before = jnp.where(row == 0, upper, pltpu.roll(value, 1, 0))
        after = jnp.where(row == rows - 1, lower, pltpu.roll(value, rows - 1, 0))
        along_y.append(0.5 * (after - before))
        before = jnp.where(column == 0, left_ref[c], pltpu.roll(value, 1, 1))
        after = jnp.where(column == width - 1, right_ref[c], pltpu.roll(value, width - 1, 1))
        along_x.append(0.5 * (after - before))
        along_z.append((0.5 / layer_pitch) * (above_ref[c] - below_ref[c]))
    nye_ref[0, 0] = -along_y[1] * mask
    nye_ref[1, 0] = -along_x[0] * mask
    nye_ref[2, 0] = -(along_x[0] + along_y[1]) * mask
    nye_ref[3, 0] = along_x[1] * mask
    nye_ref[4, 0] = along_y[0] * mask
    nye_ref[5, 0] = along_z[0] * mask
    nye_ref[6, 0] = along_z[1] * mask


def nye_of(mask, field, even, odd, left, right, below, above):
    _, rows, width = field.shape
    return pl.pallas_call(
        nye_body,
        out_shape=jax.ShapeDtypeStruct((7, 1, rows, width), F32),
        in_specs=[VMEM] * 8,
        out_specs=VMEM,
        name="nye",
    )(mask, field, even, odd, left, right, below, above)


def swap_pairs(count, start):
    pairs = []
    for i in range(start, count - 1, 2):
        pairs += [(i, i + 1), (i + 1, i)]
    return pairs


def both_sides(tail, head, axis):
    count = lax.axis_size(axis)
    return (
        lax.ppermute(tail, axis, [(i, i + 1) for i in range(count - 1)]),
        lax.ppermute(head, axis, [(i + 1, i) for i in range(count - 1)]),
    )


def on_device(frames, exponents, valid_mask):
    count = lax.axis_size("angle")
    frames = frames[0]
    exponents = exponents[0].transpose(1, 2, 0)
    sent = []
    for shift in range(1, count):
        low, high = partial_moments(frames, exponents, shift, count)
        pairs = [(i, (i + shift) % count) for i in range(count)]
        sent.append((lax.ppermute(low, "angle", pairs), lax.ppermute(high, "angle", pairs)))
    low, high = partial_moments(frames, exponents, 0, count)
    field, even, odd = field_of(low, [part[0] for part in sent])
    below, above = both_sides(field, field, "layer")
    tiles = lax.axis_size("tile")
    even = lax.ppermute(even, "tile", swap_pairs(tiles, 0))
    odd = lax.ppermute(odd, "tile", swap_pairs(tiles, 1))
    left, right = both_sides(field[:, :, -1:], field[:, :, :1], "angle")
    orient, spread = spread_of(valid_mask, field, low, high, sent)
    nye = nye_of(valid_mask, field, even, odd, left, right, below, above)
    return orient, spread, nye


def solution(mesh):
    in_specs = (
        P("layer", "angle", "tile", None),
        P("layer", "angle", "tile", None),
        P("layer", "tile", "angle"),
    )
    out_specs = (P(None, "layer", "tile", "angle"),) * 3
    return jax.shard_map(
        on_device, mesh=mesh, in_specs=in_specs, out_specs=out_specs, check_vma=False
    )
```

```python
import functools
import jax
import jax.numpy as jnp
from jax import lax
from jax.experimental import pallas as pl
from jax.experimental.pallas import tpu as pltpu
from jax.sharding import PartitionSpec as P

NPHI = 32
NCHI = 32
layer_pitch = 2.0
F32 = jnp.float32
BF16 = jnp.bfloat16
VMEM = pl.BlockSpec(memory_space=pltpu.VMEM)
ANY = pl.BlockSpec(memory_space=pltpu.HBM)


STEPS = 4


def moments_body(shift, count, steps, e_hbm, f_hbm, low_ref, high_ref, buf, ebuf, fbuf, sem, esem):
    angles, rows, width = buf.shape
    blocks = ebuf.shape[1]
    span = f_hbm.shape[2] // blocks
    here = width // span
    deep = NCHI * 8
    me = lax.axis_index("angle")
    block = lax.rem(me + shift, count)
    column = pl.multiple_of(block * width, width)
    exponent_copy = pltpu.make_async_copy(e_hbm, ebuf, esem)
    exponent_copy.start()
    size = angles // steps
    copies = []
    for step in range(steps):
        part = pl.ds(step * size, size)
        copy = pltpu.make_async_copy(
            f_hbm.at[part, :, pl.ds(column, width)], buf.at[part], sem.at[step]
        )
        copy.start()
        copies.append(copy)
    lane = lax.broadcasted_iota(jnp.int32, (8, deep), 1)
    diagonal = (lane & 7) == lax.broadcasted_iota(jnp.int32, (8, deep), 0)
    chi = ((lane >> 3).astype(F32) - 0.5 * (NCHI - 1)) / (0.5 * NCHI)
    chi_chi = chi * chi
    source = lax.broadcasted_iota(jnp.int32, (128, deep), 0)
    target = lax.broadcasted_iota(jnp.int32, (128, deep), 1) >> 3
    per = 128 // NCHI
    exponent_copy.wait()
    pieces = angles // 128
    picked = lax.broadcasted_iota(jnp.int32, (here * rows, rows * blocks), 0)
    natural = lax.broadcasted_iota(jnp.int32, (here * rows, rows * blocks), 1)
    picked = sum(
        (natural == (picked - b * rows) * blocks + block * here + b) & (picked >= b * rows) & (picked < (b + 1) * rows)
        for b in range(here)
    )
    factor = jnp.exp2(ebuf[...].reshape(rows * blocks, angles).astype(F32)).astype(BF16)
    factor = jnp.dot(picked.astype(F32).astype(BF16), factor, preferred_element_type=F32)
    factor = jnp.concatenate(
        [factor[:, c * 128 : (c + 1) * 128] for c in range(pieces)], 0
    ).astype(BF16)
    for part in range(per):
        one_hot = (source == target + NCHI * part).astype(F32).astype(BF16)
        fbuf[part] = jnp.dot(factor, one_hot, preferred_element_type=F32)
    first_phi = me * (angles // NCHI)
    groups = size // NCHI
    for step in range(steps):
        copies[step].wait()
        for r in range(rows // 8):
            at_rows = slice(r * 8, r * 8 + 8)
            for b in range(here):
                at_columns = slice(b * span, (b + 1) * span)
                left = []
                for g in range(step * groups, (step + 1) * groups):
                    phi = ((first_phi + g).astype(F32) - 0.5 * (NPHI - 1)) / (0.5 * NPHI)
                    top = ((g // per) * here + b) * rows + r * 8
                    unit = jnp.where(diagonal, fbuf[g % per, top : top + 8], 0.0)
                    left.append(
                        jnp.concatenate(
                            [
                                unit,
                                unit * phi,
                                unit * chi,
                                unit * (phi * phi),
                                unit * chi_chi,
                                unit * (phi * chi),
                            ],
                            0,
                        ).astype(BF16)
                    )
                left = jnp.concatenate(left, 1)
                cells = buf[step * size : (step + 1) * size, at_rows, at_columns].reshape(size * 8, span)
                sums = jnp.dot(left, cells, preferred_element_type=F32)
                for m in range(6):
                    ref, k = (low_ref, m) if m < 3 else (high_ref, m - 3)
                    value = sums[m * 8 : m * 8 + 8]
                    if step:
                        value = value + ref[k, at_rows, at_columns]
                    ref[k, at_rows, at_columns] = value


def partial_moments(frames, exponents, shift, count):
    angles, rows, columns = frames.shape
    width = columns // count
    steps = STEPS
    here = width * exponents.shape[1] // columns
    scratch = (angles // 128 * here * rows, NCHI * 8)
    return pl.pallas_call(
        functools.partial(moments_body, shift, count, steps),
        out_shape=[jax.ShapeDtypeStruct((3, rows, width), F32)] * 2,
        in_specs=[ANY, ANY],
        out_specs=[VMEM, VMEM],
        scratch_shapes=[
            pltpu.VMEM((angles, rows, width), BF16),
            pltpu.VMEM(exponents.shape, jnp.int32),
            pltpu.VMEM((128 // NCHI, *scratch), F32),
            pltpu.SemaphoreType.DMA((steps,)),
            pltpu.SemaphoreType.DMA,
        ],
        name=f"moments_{shift}",
        compiler_params=pltpu.CompilerParams(vmem_limit_bytes=24 << 20),
        cost_estimate=pl.CostEstimate(
            flops=512 * angles * rows * width,
            bytes_accessed=2 * angles * rows * width,
            transcendentals=0,
        ),
    )(exponents, frames)


def field_body(count, own_ref, *refs):
    parts, (field_ref, even_ref, odd_ref) = refs[: count - 1], refs[count - 1 :]
    total = own_ref[...]
    for part in parts:
        total = total + part[...]
    first = total[1] / total[0]
    second = total[2] / total[0]
    field_ref[0] = first
    field_ref[1] = second
    rows = first.shape[0]
    is_even = lax.rem(lax.axis_index("tile"), 2) == 0
    for c, value in ((0, first), (1, second)):
        head, tail = value[:1], value[rows - 1 :]
        even_ref[c] = jnp.where(is_even, tail, head)
        odd_ref[c] = jnp.where(is_even, head, tail)


def field_of(own, parts):
    _, rows, width = own.shape
    edge = jax.ShapeDtypeStruct((2, 1, width), F32)
    return pl.pallas_call(
        functools.partial(field_body, len(parts) + 1),
        out_shape=[jax.ShapeDtypeStruct((2, rows, width), F32), edge, edge],
        in_specs=[VMEM] * (len(parts) + 1),
        out_specs=[VMEM] * 3,
        name="field",
        compiler_params=pltpu.CompilerParams(vmem_limit_bytes=4 << 20),
    )(own, *parts)


def spread_body(count, mask_ref, field_ref, low_ref, high_ref, *refs):
    parts, (orient_ref, spread_ref) = refs[: 2 * count - 2], refs[2 * count - 2 :]
    mask = mask_ref[0].astype(F32)
    zeroth = low_ref[0]
    seconds = high_ref[...]
    for k in range(count - 1):
        zeroth = zeroth + parts[2 * k][0]
        seconds = seconds + parts[2 * k + 1][...]
    first, second = field_ref[0], field_ref[1]
    orient_ref[0, 0] = first * mask
    orient_ref[1, 0] = second * mask
    spread_ref[0, 0] = (seconds[0] / zeroth - first * first) * mask
    spread_ref[1, 0] = (seconds[1] / zeroth - second * second) * mask
    spread_ref[2, 0] = (seconds[2] / zeroth - first * second) * mask


def spread_of(mask, field, low, high, parts):
    _, rows, width = field.shape
    flat = [x for pair in parts for x in pair]
    return pl.pallas_call(
        functools.partial(spread_body, len(parts) + 1),
        out_shape=[
            jax.ShapeDtypeStruct((2, 1, rows, width), F32),
            jax.ShapeDtypeStruct((3, 1, rows, width), F32),
        ],
        in_specs=[VMEM] * (4 + len(flat)),
        out_specs=[VMEM] * 2,
        name="spread",
        compiler_params=pltpu.CompilerParams(vmem_limit_bytes=4 << 20),
    )(mask, field, low, high, *flat)


def nye_body(pair, mask_ref, field_ref, even_ref, odd_ref, left_ref, right_ref, below_ref, above_ref, nye_ref):
    rows, width = field_ref.shape[1:]
    mask = mask_ref[0].astype(F32)
    is_even = lax.rem(lax.axis_index("tile"), 2) == 0
    row = lax.broadcasted_iota(jnp.int32, (rows, width), 0)
    column = lax.broadcasted_iota(jnp.int32, (rows, width), 1)
    along_x, along_y, along_z = [], [], []
    for c in range(2):
        value = field_ref[c]
        upper = jnp.where(is_even, odd_ref[c], even_ref[c])
        lower = jnp.where(is_even, even_ref[c], odd_ref[c])
        before = jnp.where(row == 0, upper, pltpu.roll(value, 1, 0))
        after = jnp.where(row == rows - 1, lower, pltpu.roll(value, rows - 1, 0))
        along_y.append(0.5 * (after - before))
        before = jnp.where(column == 0, left_ref[c], pltpu.roll(value, 1, 1))
        after = jnp.where(column == width - 1, right_ref[c], pltpu.roll(value, width - 1, 1))
        along_x.append(0.5 * (after - before))
        lower_layer, upper_layer = below_ref[c], above_ref[c]
        if pair:
            is_first = lax.axis_index("layer") == 0
            lower_layer = jnp.where(is_first, 0.0, lower_layer)
            upper_layer = jnp.where(is_first, upper_layer, 0.0)
        along_z.append((0.5 / layer_pitch) * (upper_layer - lower_layer))
    nye_ref[0, 0] = -along_y[1] * mask
    nye_ref[1, 0] = -along_x[0] * mask
    nye_ref[2, 0] = -(along_x[0] + along_y[1]) * mask
    nye_ref[3, 0] = along_x[1] * mask
    nye_ref[4, 0] = along_y[0] * mask
    nye_ref[5, 0] = along_z[0] * mask
    nye_ref[6, 0] = along_z[1] * mask


def nye_of(pair, mask, field, even, odd, left, right, below, above):
    _, rows, width = field.shape
    return pl.pallas_call(
        functools.partial(nye_body, pair),
        out_shape=jax.ShapeDtypeStruct((7, 1, rows, width), F32),
        in_specs=[VMEM] * 8,
        out_specs=VMEM,
        name="nye",
        compiler_params=pltpu.CompilerParams(vmem_limit_bytes=4 << 20),
    )(mask, field, even, odd, left, right, below, above)


def swap_pairs(count, start):
    pairs = []
    for i in range(start, count - 1, 2):
        pairs += [(i, i + 1), (i + 1, i)]
    return pairs


def both_sides(tail, head, axis):
    count = lax.axis_size(axis)
    if count == 2:
        first = lax.axis_index(axis) == 0
        other = lax.ppermute(jnp.where(first, tail, head), axis, [(0, 1), (1, 0)])
        return jnp.where(first, 0.0, other), jnp.where(first, other, 0.0)
    return (
        lax.ppermute(tail, axis, [(i, i + 1) for i in range(count - 1)]),
        lax.ppermute(head, axis, [(i + 1, i) for i in range(count - 1)]),
    )


def on_device(frames, exponents, valid_mask):
    count = lax.axis_size("angle")
    frames = pltpu.with_memory_space_constraint(frames[0], pltpu.HBM)
    exponents = pltpu.with_memory_space_constraint(exponents[0].transpose(1, 2, 0), pltpu.HBM)
    sent = []
    for shift in range(1, count):
        low, high = partial_moments(frames, exponents, shift, count)
        pairs = [(i, (i + shift) % count) for i in range(count)]
        sent.append((lax.ppermute(low, "angle", pairs), lax.ppermute(high, "angle", pairs)))
    low, high = partial_moments(frames, exponents, 0, count)
    field, even, odd = field_of(low, [part[0] for part in sent])
    if lax.axis_size("layer") == 2:
        other = lax.ppermute(field, "layer", [(0, 1), (1, 0)])
        below, above = other, other
    else:
        below, above = both_sides(field, field, "layer")
    tiles = lax.axis_size("tile")
    even = lax.ppermute(even, "tile", swap_pairs(tiles, 0))
    odd = lax.ppermute(odd, "tile", swap_pairs(tiles, 1))
    left, right = both_sides(field[:, :, -1:], field[:, :, :1], "angle")
    orient, spread = spread_of(valid_mask, field, low, high, sent)
    nye = nye_of(lax.axis_size("layer") == 2, valid_mask, field, even, odd, left, right, below, above)
    return orient, spread, nye


def solution(mesh):
    in_specs = (
        P("layer", "angle", "tile", None),
        P("layer", "angle", "tile", None),
        P("layer", "tile", "angle"),
    )
    out_specs = (P(None, "layer", "tile", "angle"),) * 3
    return jax.shard_map(
        on_device, mesh=mesh, in_specs=in_specs, out_specs=out_specs, check_vma=False
    )
```

```python
import functools
import jax
import jax.numpy as jnp
from jax import lax
from jax.experimental import pallas as pl
from jax.experimental.pallas import tpu as pltpu
from jax.sharding import PartitionSpec as P

NPHI = 32
NCHI = 32
layer_pitch = 2.0
F32 = jnp.float32
BF16 = jnp.bfloat16
VMEM = pl.BlockSpec(memory_space=pltpu.VMEM)
HBM = pl.BlockSpec(memory_space=pltpu.HBM)


def moments_body(order, sizes, count, is_first, is_last, pair, *refs):
    refs = list(refs)
    f_hbm = refs.pop(0)
    e_hbm = refs.pop(0) if is_first else None
    factors, early = (None, None) if is_first else (refs.pop(0), refs.pop(0))
    if is_last and pair:
        refs.pop(0)
    low_ref, high_ref = refs.pop(0), refs.pop(0)
    if is_first:
        factors = refs.pop(0)
    ahead = None if is_last else refs.pop(0)
    edge_ref = refs.pop(0) if is_last and pair else None
    buf, sem = refs.pop(0), refs.pop(0)
    rows, width = buf.shape[1:]
    angles, _, columns = f_hbm.shape
    here = high_ref.shape[0] // 3
    span = width // here
    blocks = columns // span
    deep = NCHI * 8
    per = 128 // NCHI
    pieces = angles // 128
    shifts = list(range(1, count)) + [0]
    me = lax.axis_index("angle")

    def columns_of(k):
        block = lax.rem(me + shifts[k], count)
        return pl.ds(pl.multiple_of(block * width, width), width)

    if is_first:
        ebuf, esem = refs.pop(0), refs.pop(0)
        exponent_copy = pltpu.make_async_copy(e_hbm, ebuf, esem)
        exponent_copy.start()
    held = 0 if is_first else early.shape[0]
    copies = []
    at = held
    for step, size in enumerate(sizes):
        copy = pltpu.make_async_copy(
            f_hbm.at[pl.ds(at, size), :, columns_of(order)],
            buf.at[pl.ds(at - held, size)],
            sem.at[step],
        )
        copy.start()
        copies.append((at, size, buf, at - held, copy))
        at += size
    if not is_first:
        copies.insert(0, (0, held, early, 0, None))
    if not is_last:
        asem = refs.pop(0)
        ahead_copy = pltpu.make_async_copy(
            f_hbm.at[pl.ds(0, ahead.shape[0]), :, columns_of(order + 1)], ahead, asem
        )
        ahead_copy.start()
    lane = lax.broadcasted_iota(jnp.int32, (8, deep), 1)
    diagonal = (lane & 7) == lax.broadcasted_iota(jnp.int32, (8, deep), 0)
    chi = ((lane >> 3).astype(F32) - 0.5 * (NCHI - 1)) / (0.5 * NCHI)
    chi_chi = chi * chi
    if is_first:
        source = lax.broadcasted_iota(jnp.int32, (128, deep), 0)
        target = lax.broadcasted_iota(jnp.int32, (128, deep), 1) >> 3
        picked = lax.broadcasted_iota(jnp.int32, (rows, rows * blocks), 0)
        natural = lax.broadcasted_iota(jnp.int32, (rows, rows * blocks), 1)
        select = []
        for k in range(count):
            block = lax.rem(me + shifts[k], count)
            for b in range(here):
                select.append((natural == picked * blocks + block * here + b).astype(F32))
        select = jnp.concatenate(select, 0).astype(BF16)
        exponent_copy.wait()
        factor = jnp.exp2(ebuf[...].reshape(rows * blocks, angles).astype(F32)).astype(BF16)
        factor = jnp.dot(select, factor, preferred_element_type=F32)
        factor = jnp.concatenate(
            [factor[:, c * 128 : (c + 1) * 128] for c in range(pieces)], 0
        ).astype(BF16)
        for part in range(per):
            one_hot = (source == target + NCHI * part).astype(F32).astype(BF16)
            factors[part] = jnp.dot(factor, one_hot, preferred_element_type=F32)
    first_phi = me * (angles // NCHI)
    for start, size, where, offset, copy in copies:
        if copy is not None:
            copy.wait()
        for r in range(rows // 8):
            at_rows = slice(r * 8, r * 8 + 8)
            for b in range(here):
                at_columns = slice(b * span, (b + 1) * span)
                left = []
                for g in range(start // NCHI, (start + size) // NCHI):
                    phi = ((first_phi + g).astype(F32) - 0.5 * (NPHI - 1)) / (0.5 * NPHI)
                    top = (((g // per) * count + order) * here + b) * rows + r * 8
                    unit = jnp.where(diagonal, factors[g % per, top : top + 8], 0.0)
                    left.append(
                        jnp.concatenate(
                            [
                                unit,
                                unit * phi,
                                unit * chi,
                                unit * (phi * phi),
                                unit * chi_chi,
                                unit * (phi * chi),
                            ],
                            0,
                        ).astype(BF16)
                    )
                left = jnp.concatenate(left, 1)
                cells = where[offset : offset + size, at_rows, at_columns].reshape(size * 8, span)
                sums = jnp.dot(left, cells, preferred_element_type=F32)
                for m in range(6):
                    value = sums[m * 8 : m * 8 + 8]
                    if m < 3:
                        if start:
                            value = value + low_ref[m, at_rows, at_columns]
                        low_ref[m, at_rows, at_columns] = value
                    else:
                        if start:
                            value = value + high_ref[(m - 3) * here + b, at_rows]
                        high_ref[(m - 3) * here + b, at_rows] = value
    if edge_ref is not None:
        column = lax.broadcasted_iota(jnp.int32, (rows, 128), 1)
        slab = jnp.zeros((rows, 128), F32)
        for m in range(3):
            edge = jnp.where(me == 0, low_ref[m, :, width - 1 :], low_ref[m, :, :1])
            slab = jnp.where(column == m, edge, slab)
        edge_ref[3 * here] = slab
    if not is_last:
        ahead_copy.wait()


def step_sizes(groups, most):
    sizes = []
    while groups:
        size = min(most, max(groups // 2, 1) if groups <= most else groups)
        sizes.append(size * NCHI)
        groups -= size
    return sizes


def all_moments(frames, exponents, count, pair):
    angles, rows, columns = frames.shape
    width = columns // count
    here = width * exponents.shape[1] // columns
    span = width // here
    low_shape = jax.ShapeDtypeStruct((3, rows, width), F32)
    high_shape = jax.ShapeDtypeStruct((3 * here, rows, span), F32)
    message = jax.ShapeDtypeStruct((3 * here + 1, rows, span), F32)
    factor_shape = jax.ShapeDtypeStruct(
        (128 // NCHI, angles // 128 * count * here * rows, NCHI * 8), F32
    )
    groups = angles // NCHI
    quarter = max(groups // 4, 1)
    held = quarter * NCHI
    early_shape = jax.ShapeDtypeStruct((held, rows, width), BF16)
    sent = []
    for k in range(count):
        is_first, is_last = k == 0, k == count - 1
        sizes = step_sizes(groups if is_first else groups - quarter, quarter)
        own = 0 if is_first else held
        operands, specs, out_shape, alias = [frames], [HBM], [], {}
        scratch = [
            pltpu.VMEM((angles - own, rows, width), BF16),
            pltpu.SemaphoreType.DMA((len(sizes),)),
        ]
        if is_first:
            operands += [exponents]
            specs += [HBM]
            scratch += [pltpu.VMEM(exponents.shape, jnp.int32), pltpu.SemaphoreType.DMA]
        else:
            operands += [factors, early]
            specs += [VMEM, VMEM]
        out_shape += [low_shape, message if pair and not is_last else high_shape]
        if is_first:
            out_shape += [factor_shape]
        if not is_last:
            out_shape += [early_shape]
            scratch += [pltpu.SemaphoreType.DMA]
        if is_last and pair:
            alias = {len(operands): len(out_shape)}
            operands += [sent[0][1]]
            specs += [VMEM]
            out_shape += [message]
        out = pl.pallas_call(
            functools.partial(moments_body, k, sizes, count, is_first, is_last, pair),
            out_shape=out_shape,
            in_specs=specs,
            out_specs=[VMEM] * len(out_shape),
            scratch_shapes=scratch,
            input_output_aliases=alias,
            name=f"moments_{k}",
            compiler_params=pltpu.CompilerParams(vmem_limit_bytes=28 << 20),
            cost_estimate=pl.CostEstimate(
                flops=512 * angles * rows * width,
                bytes_accessed=2 * angles * rows * width,
                transcendentals=0,
            ),
        )(*operands)
        low, high = out[:2]
        if is_first:
            factors = out[2]
        if not is_last:
            early = out[3 if is_first else 2]
            pairs = [(i, (i + k + 1) % count) for i in range(count)]
            moved = lax.ppermute(low, "angle", pairs)
            sent.append((low, high, moved, pairs))
    highs = [entry[1] for entry in sent]
    if pair:
        highs = [out[2]]
    moved_high = [lax.ppermute(h, "angle", entry[3]) for h, entry in zip(highs, sent)]
    return low, high, [entry[2] for entry in sent], moved_high, sent[0][0]


def field_body(count, own_ref, *refs):
    parts, (field_ref, even_ref, odd_ref) = refs[: count - 1], refs[count - 1 :]
    total = own_ref[...]
    for part in parts:
        total = total + part[...]
    first = total[1] / total[0]
    second = total[2] / total[0]
    field_ref[0] = first
    field_ref[1] = second
    rows = first.shape[0]
    is_even = lax.rem(lax.axis_index("tile"), 2) == 0
    for c, value in ((0, first), (1, second)):
        head, tail = value[:1], value[rows - 1 :]
        even_ref[c] = jnp.where(is_even, tail, head)
        odd_ref[c] = jnp.where(is_even, head, tail)


def field_of(own, parts):
    _, rows, width = own.shape
    edge = jax.ShapeDtypeStruct((2, 1, width), F32)
    return pl.pallas_call(
        functools.partial(field_body, len(parts) + 1),
        out_shape=[jax.ShapeDtypeStruct((2, rows, width), F32), edge, edge],
        in_specs=[VMEM] * (len(parts) + 1),
        out_specs=[VMEM] * 3,
        name="field",
        compiler_params=pltpu.CompilerParams(vmem_limit_bytes=4 << 20),
    )(own, *parts)


def spread_body(count, mask_ref, field_ref, low_ref, high_ref, *refs):
    parts, (orient_ref, spread_ref) = refs[: 2 * count - 2], refs[2 * count - 2 :]
    here = high_ref.shape[0] // 3
    span = high_ref.shape[2]
    for b in range(here):
        at = slice(b * span, (b + 1) * span)
        mask = mask_ref[0, :, at].astype(F32)
        zeroth = low_ref[0, :, at]
        seconds = [high_ref[m * here + b] for m in range(3)]
        for k in range(count - 1):
            zeroth = zeroth + parts[2 * k][0, :, at]
            seconds = [x + parts[2 * k + 1][m * here + b] for m, x in enumerate(seconds)]
        first, second = field_ref[0, :, at], field_ref[1, :, at]
        orient_ref[0, 0, :, at] = first * mask
        orient_ref[1, 0, :, at] = second * mask
        spread_ref[0, 0, :, at] = (seconds[0] / zeroth - first * first) * mask
        spread_ref[1, 0, :, at] = (seconds[1] / zeroth - second * second) * mask
        spread_ref[2, 0, :, at] = (seconds[2] / zeroth - first * second) * mask


def spread_of(mask, field, low, high, parts):
    _, rows, width = field.shape
    flat = [x for pair in parts for x in pair]
    return pl.pallas_call(
        functools.partial(spread_body, len(parts) + 1),
        out_shape=[
            jax.ShapeDtypeStruct((2, 1, rows, width), F32),
            jax.ShapeDtypeStruct((3, 1, rows, width), F32),
        ],
        in_specs=[VMEM] * (4 + len(flat)),
        out_specs=[VMEM] * 2,
        name="spread",
        compiler_params=pltpu.CompilerParams(vmem_limit_bytes=4 << 20),
    )(mask, field, low, high, *flat)


def nye_body(two_layers, pair, mask_ref, field_ref, even_ref, odd_ref, one_ref, two_ref, below_ref, above_ref, nye_ref):
    rows, width = field_ref.shape[1:]
    mask = mask_ref[0].astype(F32)
    tile, tiles = lax.axis_index("tile"), lax.axis_size("tile")
    is_even = lax.rem(tile, 2) == 0
    row = lax.broadcasted_iota(jnp.int32, (rows, width), 0)
    column = lax.broadcasted_iota(jnp.int32, (rows, width), 1)
    along_x, along_y, along_z = [], [], []
    if pair:
        is_left = lax.axis_index("angle") == 0
        here_sums = [
            jnp.where(is_left, one_ref[m, :, :1], one_ref[m, :, width - 1 :]) for m in range(3)
        ]
        sums = [x + two_ref[two_ref.shape[0] - 1, :, m : m + 1] for m, x in enumerate(here_sums)]
    for c in range(2):
        value = field_ref[c]
        upper = jnp.where(is_even, odd_ref[c], even_ref[c])
        lower = jnp.where(is_even, even_ref[c], odd_ref[c])
        upper = jnp.where(tile == 0, 0.0, upper)
        lower = jnp.where(tile == tiles - 1, 0.0, lower)
        before = jnp.where(row == 0, upper, pltpu.roll(value, 1, 0))
        after = jnp.where(row == rows - 1, lower, pltpu.roll(value, rows - 1, 0))
        along_y.append(0.5 * (after - before))
        if pair:
            edge = sums[c + 1] / sums[0]
            left, right = jnp.where(is_left, 0.0, edge), jnp.where(is_left, edge, 0.0)
        else:
            left, right = one_ref[c], two_ref[c]
        before = jnp.where(column == 0, left, pltpu.roll(value, 1, 1))
        after = jnp.where(column == width - 1, right, pltpu.roll(value, width - 1, 1))
        along_x.append(0.5 * (after - before))
        lower_layer, upper_layer = below_ref[c], above_ref[c]
        if two_layers:
            is_first = lax.axis_index("layer") == 0
            lower_layer = jnp.where(is_first, 0.0, lower_layer)
            upper_layer = jnp.where(is_first, upper_layer, 0.0)
        along_z.append((0.5 / layer_pitch) * (upper_layer - lower_layer))
    nye_ref[0, 0] = -along_y[1] * mask
    nye_ref[1, 0] = -along_x[0] * mask
    nye_ref[2, 0] = -(along_x[0] + along_y[1]) * mask
    nye_ref[3, 0] = along_x[1] * mask
    nye_ref[4, 0] = along_y[0] * mask
    nye_ref[5, 0] = along_z[0] * mask
    nye_ref[6, 0] = along_z[1] * mask


def nye_of(two_layers, pair, *operands):
    _, rows, width = operands[1].shape
    return pl.pallas_call(
        functools.partial(nye_body, two_layers, pair),
        out_shape=jax.ShapeDtypeStruct((7, 1, rows, width), F32),
        in_specs=[VMEM] * len(operands),
        out_specs=VMEM,
        name="nye",
        compiler_params=pltpu.CompilerParams(vmem_limit_bytes=4 << 20),
    )(*operands)


def rows_exchange(message, start):
    count, tiles = lax.axis_size("angle"), lax.axis_size("tile")
    pairs = []
    for a in range(count):
        for t in range(start, tiles - 1, 2):
            i = a * tiles + t
            pairs += [(i, i + 1), (i + 1, i)]
    used = {i for i, _ in pairs}
    for a in range(0, count - 1, 2):
        for t in range(tiles):
            i, j = a * tiles + t, (a + 1) * tiles + t
            if i not in used:
                pairs += [(i, j), (j, i)]
    return lax.ppermute(message, ("angle", "tile"), pairs)


def both_sides(tail, head, axis):
    count = lax.axis_size(axis)
    return (
        lax.ppermute(tail, axis, [(i, i + 1) for i in range(count - 1)]),
        lax.ppermute(head, axis, [(i + 1, i) for i in range(count - 1)]),
    )


def on_device(frames, exponents, valid_mask):
    count = lax.axis_size("angle")
    pair = count == 2
    frames = pltpu.with_memory_space_constraint(frames[0], pltpu.HBM)
    exponents = pltpu.with_memory_space_constraint(exponents[0].transpose(1, 2, 0), pltpu.HBM)
    low, high, lows, highs, near = all_moments(frames, exponents, count, pair)
    field, even, odd = field_of(low, lows)
    two_layers = lax.axis_size("layer") == 2
    if two_layers:
        below = above = lax.ppermute(field, "layer", [(0, 1), (1, 0)])
    else:
        below, above = both_sides(field, field, "layer")
    odd = rows_exchange(odd, 1)
    even = rows_exchange(even, 0)
    if pair:
        one, two = near, highs[0]
    else:
        one, two = both_sides(field[:, :, -1:], field[:, :, :1], "angle")
    orient, spread = spread_of(valid_mask, field, low, high, list(zip(lows, highs)))
    nye = nye_of(two_layers, pair, valid_mask, field, even, odd, one, two, below, above)
    return orient, spread, nye


def solution(mesh):
    in_specs = (
        P("layer", "angle", "tile", None),
        P("layer", "angle", "tile", None),
        P("layer", "tile", "angle"),
    )
    out_specs = (P(None, "layer", "tile", "angle"),) * 3
    return jax.shard_map(
        on_device, mesh=mesh, in_specs=in_specs, out_specs=out_specs, check_vma=False
    )
```

```python
import functools
import jax
import jax.numpy as jnp
from jax import lax
from jax.experimental import pallas as pl
from jax.experimental.pallas import tpu as pltpu
from jax.sharding import PartitionSpec as P


NPHI = 32
NCHI = 32
layer_pitch = 2.0
F32 = jnp.float32
BF16 = jnp.bfloat16
VMEM = pl.BlockSpec(memory_space=pltpu.VMEM)
HBM = pl.BlockSpec(memory_space=pltpu.HBM)


def moments_body(order, sizes, count, is_first, is_last, pair, *refs):
    refs = list(refs)
    f_hbm = refs.pop(0)
    e_hbm = refs.pop(0) if is_first else None
    ebuf, early = (None, None) if is_first else (refs.pop(0), refs.pop(0))
    if is_last and pair:
        refs.pop(0)
    low_ref, high_ref = refs.pop(0), refs.pop(0)
    if is_first:
        ebuf = refs.pop(0)
    ahead = None if is_last else refs.pop(0)
    edge_ref = refs.pop(0) if is_last and pair else None
    buf, sem = refs.pop(0), refs.pop(0)
    rows, width = buf.shape[1:]
    angles, _, columns = f_hbm.shape
    here = high_ref.shape[0] // 3
    span = width // here
    blocks = columns // span
    deep = NCHI * 8
    tiles = angles // 128
    shifts = list(range(1, count)) + [0]
    me = lax.axis_index("angle")

    def columns_of(k):
        block = lax.rem(me + shifts[k], count)
        return pl.ds(pl.multiple_of(block * width, width), width)

    if is_first:
        esem = refs.pop(0)
        exponent_copy = pltpu.make_async_copy(e_hbm, ebuf, esem)
        exponent_copy.start()
    held = 0 if is_first else early.shape[0]
    copies = []
    at = held
    for step, size in enumerate(sizes):
        copy = pltpu.make_async_copy(
            f_hbm.at[pl.ds(at, size), :, columns_of(order)],
            buf.at[pl.ds(at - held, size)],
            sem.at[step],
        )
        copy.start()
        copies.append((at, size, buf, at - held, copy))
        at += size
    if not is_first:
        copies.insert(0, (0, held, early, 0, None))
    if not is_last:
        asem = refs.pop(0)
        ahead_copy = pltpu.make_async_copy(
            f_hbm.at[pl.ds(0, ahead.shape[0]), :, columns_of(order + 1)], ahead, asem
        )
        ahead_copy.start()
    lane = lax.broadcasted_iota(jnp.int32, (8, deep), 1)
    diagonal = (lane & 7) == lax.broadcasted_iota(jnp.int32, (8, deep), 0)
    chi = ((lane >> 3).astype(F32) - 0.5 * (NCHI - 1)) / (0.5 * NCHI)
    chi_chi = chi * chi
    if is_first:
        exponent_copy.wait()
    block = lax.rem(me + shifts[order], count)

    def scales(b, tile):
        top = tile * blocks + block * here + b
        return jnp.exp2(ebuf[pl.ds(top, rows, stride=tiles * blocks), :].astype(F32))

    scale_tiles = [[scales(b, tile) for tile in range(tiles)] for b in range(here)]
    gather_lane = lax.broadcasted_iota(jnp.int32, (8, 128), 1) >> 3

    def factor(b, r, g):
        piece = scale_tiles[b][g * NCHI // 128][r * 8 : r * 8 + 8]
        first = g * NCHI % 128
        return jnp.concatenate(
            [
                jnp.take_along_axis(piece, gather_lane + (first + half * 16), axis=1)
                for half in range(2)
            ],
            1,
        )

    first_phi = me * (angles // NCHI)

    def left_of(g, r):
        phi = ((first_phi + g).astype(F32) - 0.5 * (NPHI - 1)) / (0.5 * NPHI)
        left = []
        for b in range(here):
            unit = jnp.where(diagonal, factor(b, r, g), 0.0)
            left += [
                unit,
                unit * phi,
                unit * chi,
                unit * (phi * phi),
                unit * chi_chi,
                unit * (phi * chi),
            ]
        return jnp.concatenate(left, 0).astype(BF16)

    whole = rows // 8 // 2 * 2

    def unit_of(g, r):
        return r % 2 if r < whole else g % 2

    keys = sorted({(unit_of(g, r), r) for g in range(angles // NCHI) for r in range(rows // 8)})

    def accumulate(*flat):
        sums = dict(zip(keys, flat))
        turns = [0, 0]
        for start, size, where, offset, copy in copies:
            hoist = size <= 2 * NCHI
            work = [
                (g, r, left_of(g, r) if hoist else None)
                for g in range(start // NCHI, (start + size) // NCHI)
                for r in range(rows // 8)
            ]
            if copy is not None:
                copy.wait()
            for g, r, left in work:
                first = offset + g * NCHI - start
                cells = where[first : first + NCHI, r * 8 : r * 8 + 8, :].reshape(deep, width)
                unit_index = unit_of(g, r)
                stage = turns[unit_index] % 2
                turns[unit_index] += 1
                pltpu.matmul_push_rhs(cells, stage, unit_index)
                left = left_of(g, r) if left is None else left
                pltpu.matmul_acc_lhs(sums[unit_index, r], left, load_staged_rhs=stage)
        for r in range(rows // 8):
            value = sum(pltpu.matmul_pop(sums[key]) for key in keys if key[1] == r)
            at_rows = slice(r * 8, r * 8 + 8)
            for b in range(here):
                at_columns = slice(b * span, (b + 1) * span)
                for m in range(6):
                    top = (b * 6 + m) * 8
                    one = value[top : top + 8, at_columns]
                    if m < 3:
                        low_ref[m, at_rows, at_columns] = one
                    else:
                        high_ref[(m - 3) * here + b, at_rows] = one

    accumulators = [pltpu.ACC(unit)((here * 48, width), F32) for unit, _ in keys]
    pl.run_scoped(accumulate, *accumulators)
    if edge_ref is not None:
        column = lax.broadcasted_iota(jnp.int32, (rows, 128), 1)
        slab = jnp.zeros((rows, 128), F32)
        for m in range(3):
            edge = jnp.where(me == 0, low_ref[m, :, width - 1 :], low_ref[m, :, :1])
            slab = jnp.where(column == m, edge, slab)
        edge_ref[3 * here] = slab
    if not is_last:
        ahead_copy.wait()


def step_sizes(groups, most):
    sizes = []
    while groups:
        size = min(most, max(groups // 2, 1) if groups <= most else groups)
        sizes.append(size * NCHI)
        groups -= size
    return sizes


def all_moments(frames, exponents, count, pair):
    angles, rows, columns = frames.shape
    width = columns // count
    here = width * exponents.shape[0] * 128 // (columns * rows * angles)
    span = width // here
    low_shape = jax.ShapeDtypeStruct((3, rows, width), F32)
    high_shape = jax.ShapeDtypeStruct((3 * here, rows, span), F32)
    message = jax.ShapeDtypeStruct((3 * here + 1, rows, span), F32)
    groups = angles // NCHI
    quarter = max(groups // 4, 1)
    ahead_groups = max(groups // 4, 1)
    held = ahead_groups * NCHI
    early_shape = jax.ShapeDtypeStruct((held, rows, width), BF16)
    sent = []
    for k in range(count):
        is_first, is_last = k == 0, k == count - 1
        sizes = step_sizes(groups if is_first else groups - ahead_groups, quarter)
        own = 0 if is_first else held
        operands, specs, out_shape, alias = [frames], [HBM], [], {}
        scratch = [
            pltpu.VMEM((angles - own, rows, width), BF16),
            pltpu.SemaphoreType.DMA((len(sizes),)),
        ]
        if is_first:
            operands += [exponents]
            specs += [HBM]
            scratch += [pltpu.SemaphoreType.DMA]
        else:
            operands += [held_exponents, early]
            specs += [VMEM, VMEM]
        out_shape += [low_shape, message if pair and not is_last else high_shape]
        if is_first:
            out_shape += [jax.ShapeDtypeStruct(exponents.shape, jnp.int32)]
        if not is_last:
            out_shape += [early_shape]
            scratch += [pltpu.SemaphoreType.DMA]
        if is_last and pair:
            alias = {len(operands): len(out_shape)}
            operands += [sent[0][1]]
            specs += [VMEM]
            out_shape += [message]
        out = pl.pallas_call(
            functools.partial(moments_body, k, sizes, count, is_first, is_last, pair),
            out_shape=out_shape,
            in_specs=specs,
            out_specs=[VMEM] * len(out_shape),
            scratch_shapes=scratch,
            input_output_aliases=alias,
            compiler_params=pltpu.CompilerParams(vmem_limit_bytes=28 << 20),
            cost_estimate=pl.CostEstimate(
                flops=512 * angles * rows * width,
                bytes_accessed=2 * angles * rows * width,
                transcendentals=0,
            ),
        )(*operands)
        low, high = out[:2]
        if is_first:
            held_exponents = out[2]
        if not is_last:
            early = out[3 if is_first else 2]
            pairs = [(i, (i + k + 1) % count) for i in range(count)]
            moved = lax.ppermute(low, "angle", pairs)
            sent.append((low, high, moved, pairs))
    highs = [entry[1] for entry in sent]
    if pair:
        highs = [out[2]]
    moved_high = [lax.ppermute(h, "angle", entry[3]) for h, entry in zip(highs, sent)]
    return low, high, [entry[2] for entry in sent], moved_high, sent[0][0]


def field_body(count, own_ref, *refs):
    parts, (field_ref, even_ref, odd_ref) = refs[: count - 1], refs[count - 1 :]
    total = own_ref[...]
    for part in parts:
        total = total + part[...]
    first = total[1] / total[0]
    second = total[2] / total[0]
    field_ref[0] = first
    field_ref[1] = second
    rows = first.shape[0]
    is_even = lax.rem(lax.axis_index("tile"), 2) == 0
    for c, value in ((0, first), (1, second)):
        head, tail = value[:1], value[rows - 1 :]
        even_ref[c] = jnp.where(is_even, tail, head)
        odd_ref[c] = jnp.where(is_even, head, tail)


def field_of(own, parts):
    _, rows, width = own.shape
    edge = jax.ShapeDtypeStruct((2, 1, width), F32)
    return pl.pallas_call(
        functools.partial(field_body, len(parts) + 1),
        out_shape=[jax.ShapeDtypeStruct((2, rows, width), F32), edge, edge],
        in_specs=[VMEM] * (len(parts) + 1),
        out_specs=[VMEM] * 3,
        name="field",
        compiler_params=pltpu.CompilerParams(vmem_limit_bytes=4 << 20),
    )(own, *parts)


def final_body(
    count, two_layers, pair, mask_ref, field_ref, low_ref, high_ref, even_ref, odd_ref, one_ref, two_ref, below_ref, above_ref, *refs
):
    parts, (orient_ref, spread_ref, nye_ref) = refs[: 2 * count - 2], refs[2 * count - 2 :]
    rows, width = field_ref.shape[1:]
    here = high_ref.shape[0] // 3
    span = high_ref.shape[2]
    for b in range(here):
        at = slice(b * span, (b + 1) * span)
        mask = mask_ref[0, :, at].astype(F32)
        zeroth = low_ref[0, :, at]
        seconds = [high_ref[m * here + b] for m in range(3)]
        for k in range(count - 1):
            zeroth = zeroth + parts[2 * k][0, :, at]
            seconds = [x + parts[2 * k + 1][m * here + b] for m, x in enumerate(seconds)]
        first, second = field_ref[0, :, at], field_ref[1, :, at]
        orient_ref[0, 0, :, at] = first * mask
        orient_ref[1, 0, :, at] = second * mask
        spread_ref[0, 0, :, at] = (seconds[0] / zeroth - first * first) * mask
        spread_ref[1, 0, :, at] = (seconds[1] / zeroth - second * second) * mask
        spread_ref[2, 0, :, at] = (seconds[2] / zeroth - first * second) * mask
    mask = mask_ref[0].astype(F32)
    tile, tiles = lax.axis_index("tile"), lax.axis_size("tile")
    is_even = lax.rem(tile, 2) == 0
    row = lax.broadcasted_iota(jnp.int32, (rows, width), 0)
    column = lax.broadcasted_iota(jnp.int32, (rows, width), 1)
    along_x, along_y, along_z = [], [], []
    if pair:
        is_left = lax.axis_index("angle") == 0
        here_sums = [
            jnp.where(is_left, one_ref[m, :, :1], one_ref[m, :, width - 1 :]) for m in range(3)
        ]
        sums = [x + two_ref[two_ref.shape[0] - 1, :, m : m + 1] for m, x in enumerate(here_sums)]
    for c in range(2):
        value = field_ref[c]
        upper = jnp.where(is_even, odd_ref[c], even_ref[c])
        lower = jnp.where(is_even, even_ref[c], odd_ref[c])
        upper = jnp.where(tile == 0, 0.0, upper)
        lower = jnp.where(tile == tiles - 1, 0.0, lower)
        before = jnp.where(row == 0, upper, pltpu.roll(value, 1, 0))
        after = jnp.where(row == rows - 1, lower, pltpu.roll(value, rows - 1, 0))
        along_y.append(0.5 * (after - before))
        if pair:
            edge = sums[c + 1] / sums[0]
            left, right = jnp.where(is_left, 0.0, edge), jnp.where(is_left, edge, 0.0)
        else:
            left, right = one_ref[c], two_ref[c]
        before = jnp.where(column == 0, left, pltpu.roll(value, 1, 1))
        after = jnp.where(column == width - 1, right, pltpu.roll(value, width - 1, 1))
        along_x.append(0.5 * (after - before))
        lower_layer, upper_layer = below_ref[c], above_ref[c]
        if two_layers:
            is_first = lax.axis_index("layer") == 0
            lower_layer = jnp.where(is_first, 0.0, lower_layer)
            upper_layer = jnp.where(is_first, upper_layer, 0.0)
        along_z.append((0.5 / layer_pitch) * (upper_layer - lower_layer))
    nye_ref[0, 0] = -along_y[1] * mask
    nye_ref[1, 0] = -along_x[0] * mask
    nye_ref[2, 0] = -(along_x[0] + along_y[1]) * mask
    nye_ref[3, 0] = along_x[1] * mask
    nye_ref[4, 0] = along_y[0] * mask
    nye_ref[5, 0] = along_z[0] * mask
    nye_ref[6, 0] = along_z[1] * mask


def final_of(two_layers, pair, operands, parts):
    _, rows, width = operands[1].shape
    flat = [x for both in parts for x in both]
    return pl.pallas_call(
        functools.partial(final_body, len(parts) + 1, two_layers, pair),
        out_shape=[jax.ShapeDtypeStruct((n, 1, rows, width), F32) for n in (2, 3, 7)],
        in_specs=[VMEM] * (len(operands) + len(flat)),
        out_specs=[VMEM] * 3,
        name="final",
        compiler_params=pltpu.CompilerParams(vmem_limit_bytes=4 << 20),
    )(*operands, *flat)


def rows_exchange(message, start):
    tiles, layers = lax.axis_size("tile"), lax.axis_size("layer")
    pairs = []
    for j in range(layers):
        for t in range(start, tiles - 1, 2):
            i = t * layers + j
            pairs += [(i, i + layers), (i + layers, i)]
    used = {i for i, _ in pairs}
    for t in range(tiles):
        for j in range(0, layers - 1, 2):
            i = t * layers + j
            if i not in used:
                pairs += [(i, i + 1), (i + 1, i)]
    return lax.ppermute(message, ("tile", "layer"), pairs)


def both_sides(tail, head, axis):
    count = lax.axis_size(axis)
    return (
        lax.ppermute(tail, axis, [(i, i + 1) for i in range(count - 1)]),
        lax.ppermute(head, axis, [(i + 1, i) for i in range(count - 1)]),
    )


def on_device(frames, exponents, valid_mask):
    count = lax.axis_size("angle")
    pair = count == 2
    frames = pltpu.with_memory_space_constraint(frames[0], pltpu.HBM)
    angles, rows, blocks = exponents.shape[1:]
    exponents = exponents[0].reshape(angles // 128, 128, rows, blocks).transpose(2, 0, 3, 1)
    exponents = exponents.reshape(rows * angles // 128 * blocks, 128)
    exponents = pltpu.with_memory_space_constraint(exponents, pltpu.HBM)
    low, high, lows, highs, near = all_moments(frames, exponents, count, pair)
    field, even, odd = field_of(low, lows)
    two_layers = lax.axis_size("layer") == 2
    if two_layers:
        below = above = lax.ppermute(field, "layer", [(0, 1), (1, 0)])
    else:
        below, above = both_sides(field, field, "layer")
    odd = rows_exchange(odd, 1)
    even = rows_exchange(even, 0)
    if pair:
        one, two = near, highs[0]
    else:
        one, two = both_sides(field[:, :, -1:], field[:, :, :1], "angle")
    operands = [valid_mask, field, low, high, even, odd, one, two, below, above]
    return final_of(two_layers, pair, operands, list(zip(lows, highs)))


def solution(mesh):
    in_specs = (
        P("layer", "angle", "tile", None),
        P("layer", "angle", "tile", None),
        P("layer", "tile", "angle"),
    )
    out_specs = (P(None, "layer", "tile", "angle"),) * 3
    step = jax.shard_map(
        on_device, mesh=mesh, in_specs=in_specs, out_specs=out_specs, check_vma=False
    )

    def whole(*arrays):
        with jax.sharding.use_abstract_mesh(mesh.abstract_mesh):
            return step(*arrays)

    return whole
```

```python
import functools
import jax
import jax.numpy as jnp
from jax import lax
from jax.experimental import pallas as pl
from jax.experimental.pallas import tpu as pltpu
from jax.sharding import PartitionSpec as P


NPHI = 32
NCHI = 32
layer_pitch = 2.0
F32 = jnp.float32
BF16 = jnp.bfloat16
VMEM = pl.BlockSpec(memory_space=pltpu.VMEM)
HBM = pl.BlockSpec(memory_space=pltpu.HBM)


def moments_body(order, sizes, count, is_first, is_last, pair, *refs):
    refs = list(refs)
    f_hbm = refs.pop(0)
    e_hbm = refs.pop(0) if is_first else None
    ebuf, early = (None, None) if is_first else (refs.pop(0), refs.pop(0))
    if is_last and pair:
        refs.pop(0)
    low_ref, high_ref = refs.pop(0), refs.pop(0)
    if is_first:
        ebuf = refs.pop(0)
    ahead = None if is_last else refs.pop(0)
    edge_ref = refs.pop(0) if is_last and pair else None
    buf, sem = refs.pop(0), refs.pop(0)
    rows, width = buf.shape[1:]
    angles, _, columns = f_hbm.shape
    here = high_ref.shape[0] // 3
    span = width // here
    blocks = columns // span
    deep = NCHI * 8
    tiles = angles // 128
    shifts = list(range(1, count)) + [0]
    me = lax.axis_index("angle")

    def columns_of(k):
        block = lax.rem(me + shifts[k], count)
        return pl.ds(pl.multiple_of(block * width, width), width)

    if is_first:
        esem = refs.pop(0)
        exponent_copy = pltpu.make_async_copy(e_hbm, ebuf, esem)
        exponent_copy.start()
    held = 0 if is_first else early.shape[0]
    copies = []
    at = held
    for step, size in enumerate(sizes):
        copy = pltpu.make_async_copy(
            f_hbm.at[pl.ds(at, size), :, columns_of(order)],
            buf.at[pl.ds(at - held, size)],
            sem.at[step],
        )
        copy.start()
        copies.append((at, size, buf, at - held, copy))
        at += size
    if not is_first:
        copies.insert(0, (0, held, early, 0, None))
    if not is_last:
        asem = refs.pop(0)
        ahead_copy = pltpu.make_async_copy(
            f_hbm.at[pl.ds(0, ahead.shape[0]), :, columns_of(order + 1)], ahead, asem
        )
        ahead_copy.start()
    lane = lax.broadcasted_iota(jnp.int32, (8, deep), 1)
    diagonal = (lane & 7) == lax.broadcasted_iota(jnp.int32, (8, deep), 0)
    chi = ((lane >> 3).astype(F32) - 0.5 * (NCHI - 1)) / (0.5 * NCHI)
    chi_chi = chi * chi
    if is_first:
        exponent_copy.wait()
    block = lax.rem(me + shifts[order], count)

    def scales(b, tile):
        top = tile * blocks + block * here + b
        exponent = ebuf[pl.ds(top, rows, stride=tiles * blocks), :]
        return jnp.exp2(exponent.astype(F32)).astype(BF16).astype(F32)

    scale_tiles = [[scales(b, tile) for tile in range(tiles)] for b in range(here)]
    gather_lane = lax.broadcasted_iota(jnp.int32, (8, 128), 1) >> 3

    def factor(b, r, g):
        piece = scale_tiles[b][g * NCHI // 128][r * 8 : r * 8 + 8]
        first = g * NCHI % 128
        return jnp.concatenate(
            [
                jnp.take_along_axis(piece, gather_lane + (first + half * 16), axis=1)
                for half in range(2)
            ],
            1,
        )

    first_phi = me * (angles // NCHI)

    def left_of(g, r):
        phi = ((first_phi + g).astype(F32) - 0.5 * (NPHI - 1)) / (0.5 * NPHI)
        left = []
        for b in range(here):
            unit = jnp.where(diagonal, factor(b, r, g), 0.0)
            left += [
                unit,
                unit * phi,
                unit * chi,
                unit * (phi * phi),
                unit * chi_chi,
                unit * (phi * chi),
            ]
        return jnp.concatenate(left, 0).astype(BF16)

    whole = rows // 8 // 2 * 2

    def unit_of(g, r):
        return r % 2 if r < whole else g % 2

    keys = sorted({(unit_of(g, r), r) for g in range(angles // NCHI) for r in range(rows // 8)})

    def accumulate(*flat):
        sums = dict(zip(keys, flat))
        turns = [0, 0]
        for start, size, where, offset, copy in copies:
            hoist = size <= 2 * NCHI
            work = [
                (g, r, left_of(g, r) if hoist else None)
                for g in range(start // NCHI, (start + size) // NCHI)
                for r in range(rows // 8)
            ]
            if copy is not None:
                copy.wait()
            for g, r, left in work:
                first = offset + g * NCHI - start
                cells = where[first : first + NCHI, r * 8 : r * 8 + 8, :].reshape(deep, width)
                unit_index = unit_of(g, r)
                stage = turns[unit_index] % 2
                turns[unit_index] += 1
                pltpu.matmul_push_rhs(cells, stage, unit_index)
                left = left_of(g, r) if left is None else left
                pltpu.matmul_acc_lhs(sums[unit_index, r], left, load_staged_rhs=stage)
        for r in range(rows // 8):
            value = sum(pltpu.matmul_pop(sums[key]) for key in keys if key[1] == r)
            at_rows = slice(r * 8, r * 8 + 8)
            for b in range(here):
                at_columns = slice(b * span, (b + 1) * span)
                for m in range(6):
                    top = (b * 6 + m) * 8
                    one = value[top : top + 8, at_columns]
                    if m < 3:
                        low_ref[m, at_rows, at_columns] = one
                    else:
                        high_ref[(m - 3) * here + b, at_rows] = one

    accumulators = [pltpu.ACC(unit)((here * 48, width), F32) for unit, _ in keys]
    pl.run_scoped(accumulate, *accumulators)
    if edge_ref is not None:
        column = lax.broadcasted_iota(jnp.int32, (rows, 128), 1)
        slab = jnp.zeros((rows, 128), F32)
        for m in range(3):
            edge = jnp.where(me == 0, low_ref[m, :, width - 1 :], low_ref[m, :, :1])
            slab = jnp.where(column == m, edge, slab)
        edge_ref[3 * here] = slab
    if not is_last:
        ahead_copy.wait()


def step_sizes(groups, most):
    sizes = []
    while groups:
        size = most if groups > most else max(groups // 2, min(groups, 2))
        sizes.append(size * NCHI)
        groups -= size
    return sizes


def all_moments(frames, exponents, count, pair):
    angles, rows, columns = frames.shape
    width = columns // count
    here = width * exponents.shape[0] * 128 // (columns * rows * angles)
    span = width // here
    low_shape = jax.ShapeDtypeStruct((3, rows, width), F32)
    high_shape = jax.ShapeDtypeStruct((3 * here, rows, span), F32)
    message = jax.ShapeDtypeStruct((3 * here + 1, rows, span), F32)
    groups = angles // NCHI
    quarter = max(groups // 4, 1)
    ahead_groups = max(groups // 4, 1)
    held = ahead_groups * NCHI
    early_shape = jax.ShapeDtypeStruct((held, rows, width), BF16)
    sent = []
    for k in range(count):
        is_first, is_last = k == 0, k == count - 1
        sizes = step_sizes(groups if is_first else groups - ahead_groups, quarter)
        own = 0 if is_first else held
        operands, specs, out_shape, alias = [frames], [HBM], [], {}
        scratch = [
            pltpu.VMEM((angles - own, rows, width), BF16),
            pltpu.SemaphoreType.DMA((len(sizes),)),
        ]
        if is_first:
            operands += [exponents]
            specs += [HBM]
            scratch += [pltpu.SemaphoreType.DMA]
        else:
            operands += [held_exponents, early]
            specs += [VMEM, VMEM]
        out_shape += [low_shape, message if pair and not is_last else high_shape]
        if is_first:
            out_shape += [jax.ShapeDtypeStruct(exponents.shape, jnp.int32)]
        if not is_last:
            out_shape += [early_shape]
            scratch += [pltpu.SemaphoreType.DMA]
        if is_last and pair:
            alias = {len(operands): len(out_shape)}
            operands += [sent[0][1]]
            specs += [VMEM]
            out_shape += [message]
        out = pl.pallas_call(
            functools.partial(moments_body, k, sizes, count, is_first, is_last, pair),
            out_shape=out_shape,
            in_specs=specs,
            out_specs=[VMEM] * len(out_shape),
            scratch_shapes=scratch,
            input_output_aliases=alias,
            compiler_params=pltpu.CompilerParams(vmem_limit_bytes=28 << 20),
            cost_estimate=pl.CostEstimate(
                flops=512 * angles * rows * width,
                bytes_accessed=2 * angles * rows * width,
                transcendentals=0,
            ),
        )(*operands)
        low, high = out[:2]
        if is_first:
            held_exponents = out[2]
        if not is_last:
            early = out[3 if is_first else 2]
            pairs = [(i, (i + k + 1) % count) for i in range(count)]
            moved = lax.ppermute(low, "angle", pairs)
            sent.append((low, high, moved, pairs))
    highs = [entry[1] for entry in sent]
    if pair:
        highs = [out[2]]
    moved_high = [lax.ppermute(h, "angle", entry[3]) for h, entry in zip(highs, sent)]
    return low, high, [entry[2] for entry in sent], moved_high, sent[0][0]


def field_body(count, own_ref, *refs):
    parts, (field_ref, even_ref, odd_ref) = refs[: count - 1], refs[count - 1 :]
    total = own_ref[...]
    for part in parts:
        total = total + part[...]
    first = total[1] / total[0]
    second = total[2] / total[0]
    field_ref[0] = first
    field_ref[1] = second
    rows = first.shape[0]
    is_even = lax.rem(lax.axis_index("tile"), 2) == 0
    for c, value in ((0, first), (1, second)):
        head, tail = value[:1], value[rows - 1 :]
        even_ref[c] = jnp.where(is_even, tail, head)
        odd_ref[c] = jnp.where(is_even, head, tail)


def field_of(own, parts):
    _, rows, width = own.shape
    edge = jax.ShapeDtypeStruct((2, 1, width), F32)
    return pl.pallas_call(
        functools.partial(field_body, len(parts) + 1),
        out_shape=[jax.ShapeDtypeStruct((2, rows, width), F32), edge, edge],
        in_specs=[VMEM] * (len(parts) + 1),
        out_specs=[VMEM] * 3,
        name="field",
        compiler_params=pltpu.CompilerParams(vmem_limit_bytes=4 << 20),
    )(own, *parts)


def final_body(
    count, two_layers, pair, mask_ref, field_ref, low_ref, high_ref, even_ref, odd_ref, one_ref, two_ref, below_ref, above_ref, *refs
):
    parts, (orient_ref, spread_ref, nye_ref) = refs[: 2 * count - 2], refs[2 * count - 2 :]
    rows, width = field_ref.shape[1:]
    here = high_ref.shape[0] // 3
    span = high_ref.shape[2]
    for b in range(here):
        at = slice(b * span, (b + 1) * span)
        mask = mask_ref[0, :, at].astype(F32)
        zeroth = low_ref[0, :, at]
        seconds = [high_ref[m * here + b] for m in range(3)]
        for k in range(count - 1):
            zeroth = zeroth + parts[2 * k][0, :, at]
            seconds = [x + parts[2 * k + 1][m * here + b] for m, x in enumerate(seconds)]
        first, second = field_ref[0, :, at], field_ref[1, :, at]
        orient_ref[0, 0, :, at] = first * mask
        orient_ref[1, 0, :, at] = second * mask
        spread_ref[0, 0, :, at] = (seconds[0] / zeroth - first * first) * mask
        spread_ref[1, 0, :, at] = (seconds[1] / zeroth - second * second) * mask
        spread_ref[2, 0, :, at] = (seconds[2] / zeroth - first * second) * mask
    mask = mask_ref[0].astype(F32)
    tile, tiles = lax.axis_index("tile"), lax.axis_size("tile")
    is_even = lax.rem(tile, 2) == 0
    row = lax.broadcasted_iota(jnp.int32, (rows, width), 0)
    column = lax.broadcasted_iota(jnp.int32, (rows, width), 1)
    along_x, along_y, along_z = [], [], []
    if pair:
        is_left = lax.axis_index("angle") == 0
        here_sums = [
            jnp.where(is_left, one_ref[m, :, :1], one_ref[m, :, width - 1 :]) for m in range(3)
        ]
        sums = [x + two_ref[two_ref.shape[0] - 1, :, m : m + 1] for m, x in enumerate(here_sums)]
    for c in range(2):
        value = field_ref[c]
        upper = jnp.where(is_even, odd_ref[c], even_ref[c])
        lower = jnp.where(is_even, even_ref[c], odd_ref[c])
        upper = jnp.where(tile == 0, 0.0, upper)
        lower = jnp.where(tile == tiles - 1, 0.0, lower)
        before = jnp.where(row == 0, upper, pltpu.roll(value, 1, 0))
        after = jnp.where(row == rows - 1, lower, pltpu.roll(value, rows - 1, 0))
        along_y.append(0.5 * (after - before))
        if pair:
            edge = sums[c + 1] / sums[0]
            left, right = jnp.where(is_left, 0.0, edge), jnp.where(is_left, edge, 0.0)
        else:
            left, right = one_ref[c], two_ref[c]
        before = jnp.where(column == 0, left, pltpu.roll(value, 1, 1))
        after = jnp.where(column == width - 1, right, pltpu.roll(value, width - 1, 1))
        along_x.append(0.5 * (after - before))
        lower_layer, upper_layer = below_ref[c], above_ref[c]
        if two_layers:
            is_first = lax.axis_index("layer") == 0
            lower_layer = jnp.where(is_first, 0.0, lower_layer)
            upper_layer = jnp.where(is_first, upper_layer, 0.0)
        along_z.append((0.5 / layer_pitch) * (upper_layer - lower_layer))
    nye_ref[0, 0] = -along_y[1] * mask
    nye_ref[1, 0] = -along_x[0] * mask
    nye_ref[2, 0] = -(along_x[0] + along_y[1]) * mask
    nye_ref[3, 0] = along_x[1] * mask
    nye_ref[4, 0] = along_y[0] * mask
    nye_ref[5, 0] = along_z[0] * mask
    nye_ref[6, 0] = along_z[1] * mask


def final_of(two_layers, pair, operands, parts):
    _, rows, width = operands[1].shape
    flat = [x for both in parts for x in both]
    return pl.pallas_call(
        functools.partial(final_body, len(parts) + 1, two_layers, pair),
        out_shape=[jax.ShapeDtypeStruct((n, 1, rows, width), F32) for n in (2, 3, 7)],
        in_specs=[VMEM] * (len(operands) + len(flat)),
        out_specs=[VMEM] * 3,
        name="final",
        compiler_params=pltpu.CompilerParams(vmem_limit_bytes=4 << 20),
    )(*operands, *flat)


def rows_exchange(message, start):
    tiles, layers = lax.axis_size("tile"), lax.axis_size("layer")
    pairs = []
    for j in range(layers):
        for t in range(start, tiles - 1, 2):
            i = t * layers + j
            pairs += [(i, i + layers), (i + layers, i)]
    used = {i for i, _ in pairs}
    for t in range(tiles):
        for j in range(0, layers - 1, 2):
            i = t * layers + j
            if i not in used:
                pairs += [(i, i + 1), (i + 1, i)]
    return lax.ppermute(message, ("tile", "layer"), pairs)


def both_sides(tail, head, axis):
    count = lax.axis_size(axis)
    return (
        lax.ppermute(tail, axis, [(i, i + 1) for i in range(count - 1)]),
        lax.ppermute(head, axis, [(i + 1, i) for i in range(count - 1)]),
    )


def on_device(frames, exponents, valid_mask):
    count = lax.axis_size("angle")
    pair = count == 2
    frames = pltpu.with_memory_space_constraint(frames[0], pltpu.HBM)
    angles, rows, blocks = exponents.shape[1:]
    exponents = exponents[0].reshape(angles // 128, 128, rows, blocks).transpose(2, 0, 3, 1)
    exponents = exponents.reshape(rows * angles // 128 * blocks, 128)
    exponents = pltpu.with_memory_space_constraint(exponents, pltpu.HBM)
    low, high, lows, highs, near = all_moments(frames, exponents, count, pair)
    field, even, odd = field_of(low, lows)
    two_layers = lax.axis_size("layer") == 2
    if two_layers:
        below = above = lax.ppermute(field, "layer", [(0, 1), (1, 0)])
    else:
        below, above = both_sides(field, field, "layer")
    odd = rows_exchange(odd, 1)
    even = rows_exchange(even, 0)
    if pair:
        one, two = near, highs[0]
    else:
        one, two = both_sides(field[:, :, -1:], field[:, :, :1], "angle")
    operands = [valid_mask, field, low, high, even, odd, one, two, below, above]
    return final_of(two_layers, pair, operands, list(zip(lows, highs)))


def solution(mesh):
    in_specs = (
        P("layer", "angle", "tile", None),
        P("layer", "angle", "tile", None),
        P("layer", "tile", "angle"),
    )
    out_specs = (P(None, "layer", "tile", "angle"),) * 3
    step = jax.shard_map(
        on_device, mesh=mesh, in_specs=in_specs, out_specs=out_specs, check_vma=False
    )

    def whole(*arrays):
        with jax.sharding.use_abstract_mesh(mesh.abstract_mesh):
            return step(*arrays)

    return whole
```

```python
import functools
import jax
import jax.numpy as jnp
from jax import lax
from jax.experimental import pallas as pl
from jax.experimental.pallas import tpu as pltpu
from jax.sharding import PartitionSpec as P


NPHI = 32
NCHI = 32
layer_pitch = 2.0
F32 = jnp.float32
BF16 = jnp.bfloat16
VMEM = pl.BlockSpec(memory_space=pltpu.VMEM)
HBM = pl.BlockSpec(memory_space=pltpu.HBM)


def moments_body(order, sizes, count, is_first, is_last, pair, *refs):
    refs = list(refs)
    f_hbm = refs.pop(0)
    e_hbm = refs.pop(0) if is_first else None
    ebuf, early = (None, None) if is_first else (refs.pop(0), refs.pop(0))
    if is_last and pair:
        refs.pop(0)
    low_ref, high_ref = refs.pop(0), refs.pop(0)
    if is_first:
        ebuf = refs.pop(0)
    ahead = None if is_last else refs.pop(0)
    edge_ref = refs.pop(0) if is_last and pair else None
    buf, sem = refs.pop(0), refs.pop(0)
    rows, width = buf.shape[1:]
    angles, _, columns = f_hbm.shape
    here = high_ref.shape[0] // 3
    span = width // here
    blocks = columns // span
    deep = NCHI * 8
    tiles = angles // 128
    shifts = list(range(1, count)) + [0]
    me = lax.axis_index("angle")

    def columns_of(k):
        block = lax.rem(me + shifts[k], count)
        return pl.ds(pl.multiple_of(block * width, width), width)

    if is_first:
        esem = refs.pop(0)
        exponent_copy = pltpu.make_async_copy(e_hbm, ebuf, esem)
        exponent_copy.start()
    held = 0 if is_first else early.shape[0]
    copies = []
    at = held
    for step, size in enumerate(sizes):
        copy = pltpu.make_async_copy(
            f_hbm.at[pl.ds(at, size), :, columns_of(order)],
            buf.at[pl.ds(at - held, size)],
            sem.at[step],
        )
        copy.start()
        copies.append((at, size, buf, at - held, copy))
        at += size
    if not is_first:
        copies.insert(0, (0, held, early, 0, None))
    if not is_last:
        asem = refs.pop(0)
        ahead_copy = pltpu.make_async_copy(
            f_hbm.at[pl.ds(0, ahead.shape[0]), :, columns_of(order + 1)], ahead, asem
        )
        ahead_copy.start()
    lane = lax.broadcasted_iota(jnp.int32, (8, deep), 1)
    diagonal = (lane & 7) == lax.broadcasted_iota(jnp.int32, (8, deep), 0)
    chi = ((lane >> 3).astype(F32) - 0.5 * (NCHI - 1)) / (0.5 * NCHI)
    chi_chi = chi * chi
    if is_first:
        exponent_copy.wait()
    block = lax.rem(me + shifts[order], count)

    def scales(b, tile):
        top = tile * blocks + block * here + b
        exponent = ebuf[pl.ds(top, rows, stride=tiles * blocks), :]
        return jnp.exp2(exponent.astype(F32)).astype(BF16).astype(F32)

    scale_tiles = [[scales(b, tile) for tile in range(tiles)] for b in range(here)]
    gather_lane = lax.broadcasted_iota(jnp.int32, (8, 128), 1) >> 3

    def factor(b, r, g):
        piece = scale_tiles[b][g * NCHI // 128][r * 8 : r * 8 + 8]
        first = g * NCHI % 128
        return jnp.concatenate(
            [
                jnp.take_along_axis(piece, gather_lane + (first + half * 16), axis=1)
                for half in range(2)
            ],
            1,
        )

    first_phi = me * (angles // NCHI)

    def left_of(g, r):
        phi = ((first_phi + g).astype(F32) - 0.5 * (NPHI - 1)) / (0.5 * NPHI)
        left = []
        for b in range(here):
            unit = jnp.where(diagonal, factor(b, r, g), 0.0)
            left += [
                unit,
                unit * phi,
                unit * chi,
                unit * (phi * phi),
                unit * chi_chi,
                unit * (phi * chi),
            ]
        return jnp.concatenate(left, 0).astype(BF16)

    whole = rows // 8 // 2 * 2

    def unit_of(g, r):
        return r % 2 if r < whole else g % 2

    keys = sorted({(unit_of(g, r), r) for g in range(angles // NCHI) for r in range(rows // 8)})

    def accumulate(*flat):
        sums = dict(zip(keys, flat))
        turns = [0, 0]
        for start, size, where, offset, copy in copies:
            hoist = size <= 2 * NCHI
            work = [
                (g, r, left_of(g, r) if hoist else None)
                for g in range(start // NCHI, (start + size) // NCHI)
                for r in range(rows // 8)
            ]
            if copy is not None:
                copy.wait()
            for g, r, left in work:
                first = offset + g * NCHI - start
                cells = where[first : first + NCHI, r * 8 : r * 8 + 8, :].reshape(deep, width)
                unit_index = unit_of(g, r)
                stage = turns[unit_index] % 2
                turns[unit_index] += 1
                pltpu.matmul_push_rhs(cells, stage, unit_index)
                left = left_of(g, r) if left is None else left
                pltpu.matmul_acc_lhs(sums[unit_index, r], left, load_staged_rhs=stage)
        for r in range(rows // 8):
            value = sum(pltpu.matmul_pop(sums[key]) for key in keys if key[1] == r)
            at_rows = slice(r * 8, r * 8 + 8)
            for b in range(here):
                at_columns = slice(b * span, (b + 1) * span)
                for m in range(6):
                    top = (b * 6 + m) * 8
                    one = value[top : top + 8, at_columns]
                    if m < 3:
                        low_ref[m, at_rows, at_columns] = one
                    else:
                        high_ref[(m - 3) * here + b, at_rows] = one

    accumulators = [pltpu.ACC(unit)((here * 48, width), F32) for unit, _ in keys]
    pl.run_scoped(accumulate, *accumulators)
    if edge_ref is not None:
        column = lax.broadcasted_iota(jnp.int32, (rows, 128), 1)
        slab = jnp.zeros((rows, 128), F32)
        for m in range(3):
            edge = jnp.where(me == 0, low_ref[m, :, width - 1 :], low_ref[m, :, :1])
            slab = jnp.where(column == m, edge, slab)
        edge_ref[3 * here] = slab
    if not is_last:
        ahead_copy.wait()


def step_sizes(groups, most):
    sizes = []
    while groups:
        size = most if groups > most else max(groups // 2, min(groups, 2))
        sizes.append(size * NCHI)
        groups -= size
    return sizes


def all_moments(frames, exponents, count, pair):
    angles, rows, columns = frames.shape
    width = columns // count
    here = width * exponents.shape[0] * 128 // (columns * rows * angles)
    span = width // here
    low_shape = jax.ShapeDtypeStruct((3, rows, width), F32)
    high_shape = jax.ShapeDtypeStruct((3 * here, rows, span), F32)
    message = jax.ShapeDtypeStruct((3 * here + 1, rows, span), F32)
    groups = angles // NCHI
    quarter = max(groups // 4, 1)
    ahead_groups = max(groups // 4, 1)
    held = ahead_groups * NCHI
    early_shape = jax.ShapeDtypeStruct((held, rows, width), BF16)
    sent = []
    for k in range(count):
        is_first, is_last = k == 0, k == count - 1
        sizes = step_sizes(groups if is_first else groups - ahead_groups, quarter)
        own = 0 if is_first else held
        operands, specs, out_shape, alias = [frames], [HBM], [], {}
        scratch = [
            pltpu.VMEM((angles - own, rows, width), BF16),
            pltpu.SemaphoreType.DMA((len(sizes),)),
        ]
        if is_first:
            operands += [exponents]
            specs += [HBM]
            scratch += [pltpu.SemaphoreType.DMA]
        else:
            operands += [held_exponents, early]
            specs += [VMEM, VMEM]
        out_shape += [low_shape, message if pair and not is_last else high_shape]
        if is_first:
            out_shape += [jax.ShapeDtypeStruct(exponents.shape, jnp.int32)]
        if not is_last:
            out_shape += [early_shape]
            scratch += [pltpu.SemaphoreType.DMA]
        if is_last and pair:
            alias = {len(operands): len(out_shape)}
            operands += [sent[0][1]]
            specs += [VMEM]
            out_shape += [message]
        out = pl.pallas_call(
            functools.partial(moments_body, k, sizes, count, is_first, is_last, pair),
            out_shape=out_shape,
            in_specs=specs,
            out_specs=[VMEM] * len(out_shape),
            scratch_shapes=scratch,
            input_output_aliases=alias,
            compiler_params=pltpu.CompilerParams(vmem_limit_bytes=28 << 20),
            cost_estimate=pl.CostEstimate(
                flops=512 * angles * rows * width,
                bytes_accessed=2 * angles * rows * width,
                transcendentals=0,
            ),
        )(*operands)
        low, high = out[:2]
        if is_first:
            held_exponents = out[2]
        if not is_last:
            early = out[3 if is_first else 2]
            pairs = [(i, (i + k + 1) % count) for i in range(count)]
            moved = lax.ppermute(low, "angle", pairs)
            sent.append((low, high, moved, pairs))
    highs = [entry[1] for entry in sent]
    if pair:
        highs = [out[2]]
    moved_high = [lax.ppermute(h, "angle", entry[3]) for h, entry in zip(highs, sent)]
    return low, high, [entry[2] for entry in sent], moved_high, sent[0][0]


def field_body(count, own_ref, *refs):
    parts, (field_ref, even_ref, odd_ref) = refs[: count - 1], refs[count - 1 :]
    total = own_ref[...]
    for part in parts:
        total = total + part[...]
    first = total[1] / total[0]
    second = total[2] / total[0]
    field_ref[0] = first
    field_ref[1] = second
    rows = first.shape[0]
    is_even = lax.rem(lax.axis_index("tile"), 2) == 0
    for c, value in ((0, first), (1, second)):
        head, tail = value[:1], value[rows - 1 :]
        even_ref[c] = jnp.where(is_even, tail, head)
        odd_ref[c] = jnp.where(is_even, head, tail)


def field_of(own, parts):
    _, rows, width = own.shape
    edge = jax.ShapeDtypeStruct((2, 1, width), F32)
    return pl.pallas_call(
        functools.partial(field_body, len(parts) + 1),
        out_shape=[jax.ShapeDtypeStruct((2, rows, width), F32), edge, edge],
        in_specs=[VMEM] * (len(parts) + 1),
        out_specs=[VMEM] * 3,
        name="field",
        compiler_params=pltpu.CompilerParams(vmem_limit_bytes=4 << 20),
    )(own, *parts)


def final_body(
    count, two_layers, pair, mask_ref, field_ref, low_ref, high_ref, even_ref, odd_ref, one_ref, two_ref, below_ref, above_ref, *refs
):
    parts, refs = refs[: 2 * count - 2], refs[2 * count - 2 :]
    orient_out, spread_out, nye_out, orient_ref, spread_ref, nye_ref, sem = refs
    rows, width = field_ref.shape[1:]
    copies = []

    def send(source, target):
        copy = pltpu.make_async_copy(source, target, sem.at[len(copies)])
        copy.start()
        copies.append(copy)

    here = high_ref.shape[0] // 3
    span = high_ref.shape[2]
    for b in range(here):
        at = slice(b * span, (b + 1) * span)
        mask = mask_ref[0, :, at].astype(F32)
        zeroth = low_ref[0, :, at]
        seconds = [high_ref[m * here + b] for m in range(3)]
        for k in range(count - 1):
            zeroth = zeroth + parts[2 * k][0, :, at]
            seconds = [x + parts[2 * k + 1][m * here + b] for m, x in enumerate(seconds)]
        first, second = field_ref[0, :, at], field_ref[1, :, at]
        orient_ref[0, 0, :, at] = first * mask
        orient_ref[1, 0, :, at] = second * mask
        spread_ref[0, 0, :, at] = (seconds[0] / zeroth - first * first) * mask
        spread_ref[1, 0, :, at] = (seconds[1] / zeroth - second * second) * mask
        spread_ref[2, 0, :, at] = (seconds[2] / zeroth - first * second) * mask
    send(orient_ref, orient_out)
    send(spread_ref, spread_out)
    mask = mask_ref[0].astype(F32)
    for c in range(2):
        lower_layer, upper_layer = below_ref[c], above_ref[c]
        if two_layers:
            is_first = lax.axis_index("layer") == 0
            lower_layer = jnp.where(is_first, 0.0, lower_layer)
            upper_layer = jnp.where(is_first, upper_layer, 0.0)
        nye_ref[5 + c, 0] = (0.5 / layer_pitch) * (upper_layer - lower_layer) * mask
    send(nye_ref.at[pl.ds(5, 2)], nye_out.at[pl.ds(5, 2)])
    tile, tiles = lax.axis_index("tile"), lax.axis_size("tile")
    is_even = lax.rem(tile, 2) == 0
    row = lax.broadcasted_iota(jnp.int32, (rows, width), 0)
    column = lax.broadcasted_iota(jnp.int32, (rows, width), 1)
    along_x, along_y = [], []
    if pair:
        is_left = lax.axis_index("angle") == 0
        here_sums = [
            jnp.where(is_left, one_ref[m, :, :1], one_ref[m, :, width - 1 :]) for m in range(3)
        ]
        sums = [x + two_ref[two_ref.shape[0] - 1, :, m : m + 1] for m, x in enumerate(here_sums)]
    for c in range(2):
        value = field_ref[c]
        upper = jnp.where(is_even, odd_ref[c], even_ref[c])
        lower = jnp.where(is_even, even_ref[c], odd_ref[c])
        upper = jnp.where(tile == 0, 0.0, upper)
        lower = jnp.where(tile == tiles - 1, 0.0, lower)
        before = jnp.where(row == 0, upper, pltpu.roll(value, 1, 0))
        after = jnp.where(row == rows - 1, lower, pltpu.roll(value, rows - 1, 0))
        along_y.append(0.5 * (after - before))
        if pair:
            edge = sums[c + 1] / sums[0]
            left, right = jnp.where(is_left, 0.0, edge), jnp.where(is_left, edge, 0.0)
        else:
            left, right = one_ref[c], two_ref[c]
        before = jnp.where(column == 0, left, pltpu.roll(value, 1, 1))
        after = jnp.where(column == width - 1, right, pltpu.roll(value, width - 1, 1))
        along_x.append(0.5 * (after - before))
    nye_ref[0, 0] = -along_y[1] * mask
    nye_ref[1, 0] = -along_x[0] * mask
    nye_ref[2, 0] = -(along_x[0] + along_y[1]) * mask
    nye_ref[3, 0] = along_x[1] * mask
    nye_ref[4, 0] = along_y[0] * mask
    send(nye_ref.at[pl.ds(0, 5)], nye_out.at[pl.ds(0, 5)])
    for copy in copies:
        copy.wait()


def final_of(two_layers, pair, operands, parts):
    _, rows, width = operands[1].shape
    flat = [x for both in parts for x in both]
    return pl.pallas_call(
        functools.partial(final_body, len(parts) + 1, two_layers, pair),
        out_shape=[jax.ShapeDtypeStruct((n, 1, rows, width), F32) for n in (2, 3, 7)],
        in_specs=[VMEM] * (len(operands) + len(flat)),
        out_specs=[HBM] * 3,
        scratch_shapes=[pltpu.VMEM((n, 1, rows, width), F32) for n in (2, 3, 7)]
        + [pltpu.SemaphoreType.DMA((4,))],
        name="final",
        compiler_params=pltpu.CompilerParams(vmem_limit_bytes=4 << 20),
    )(*operands, *flat)


def rows_exchange(message, start):
    tiles, layers = lax.axis_size("tile"), lax.axis_size("layer")
    pairs = []
    for j in range(layers):
        for t in range(start, tiles - 1, 2):
            i = t * layers + j
            pairs += [(i, i + layers), (i + layers, i)]
    used = {i for i, _ in pairs}
    for t in range(tiles):
        for j in range(0, layers - 1, 2):
            i = t * layers + j
            if i not in used:
                pairs += [(i, i + 1), (i + 1, i)]
    return lax.ppermute(message, ("tile", "layer"), pairs)


def both_sides(tail, head, axis):
    count = lax.axis_size(axis)
    return (
        lax.ppermute(tail, axis, [(i, i + 1) for i in range(count - 1)]),
        lax.ppermute(head, axis, [(i + 1, i) for i in range(count - 1)]),
    )


def on_device(frames, exponents, valid_mask):
    count = lax.axis_size("angle")
    pair = count == 2
    frames = pltpu.with_memory_space_constraint(frames[0], pltpu.HBM)
    angles, rows, blocks = exponents.shape[1:]
    exponents = exponents[0].reshape(angles // 128, 128, rows, blocks).transpose(2, 0, 3, 1)
    exponents = exponents.reshape(rows * angles // 128 * blocks, 128)
    exponents = pltpu.with_memory_space_constraint(exponents, pltpu.HBM)
    low, high, lows, highs, near = all_moments(frames, exponents, count, pair)
    field, even, odd = field_of(low, lows)
    two_layers = lax.axis_size("layer") == 2
    if two_layers:
        below = above = lax.ppermute(field, "layer", [(0, 1), (1, 0)])
    else:
        below, above = both_sides(field, field, "layer")
    odd = rows_exchange(odd, 1)
    even = rows_exchange(even, 0)
    if pair:
        one, two = near, highs[0]
    else:
        one, two = both_sides(field[:, :, -1:], field[:, :, :1], "angle")
    operands = [valid_mask, field, low, high, even, odd, one, two, below, above]
    return final_of(two_layers, pair, operands, list(zip(lows, highs)))


def solution(mesh):
    in_specs = (
        P("layer", "angle", "tile", None),
        P("layer", "angle", "tile", None),
        P("layer", "tile", "angle"),
    )
    out_specs = (P(None, "layer", "tile", "angle"),) * 3
    step = jax.shard_map(
        on_device, mesh=mesh, in_specs=in_specs, out_specs=out_specs, check_vma=False
    )

    def whole(*arrays):
        with jax.sharding.use_abstract_mesh(mesh.abstract_mesh):
            return step(*arrays)

    return whole
```
